256 devices in a mesh: seq: 64 (over x, z, core), tp: 4 (over y).
Axes of the slice: x: 4, y: 4, z: 8, core: 2. Of those that a mesh axis runs over, the one named last changes fastest.
Arguments:
- hidden: bfloat16 [32768, 4608], P('seq', 'tp'), may hold values from -60 to 60, as said below
- norm_gain: float32 [4608], replicated, may hold values from 0.1 to 1.9
- w_query: bfloat16 [4608, 2048], P(None, 'tp'), may hold values from -0.25 to 0.25
- w_key: bfloat16 [4608, 1024], P(None, 'tp'), may hold values from -0.09375 to 0.09375
- w_value: bfloat16 [4608, 1024], P(None, 'tp'), may hold values from -0.09375 to 0.09375
- segment_ids: int32 [32768], P('seq'), may hold values from 0 to 15, as said below
- page_table: int32 [64, 4], P('seq'), may hold values from 0 to 3, each once within a row
Outputs:
- attended: bfloat16 [32768, 2048], P('seq', 'tp')
- kv_cache: bfloat16 [256, 128, 2, 1024], P(('seq', 'tp'))
The draws below stay inside these ranges and needn't reach their ends.
Inputs may be any that keep to these rules, and one draw needn't show every extreme that they name: hidden is finite. `segment_ids`: never falling along the stream and rising by one at each document start; every number from 0 to 15 appears; no document is longer than 4096 tokens. `page_table`: each row holds every number from 0 to 3 once.
All inputs are finite; a program needn't handle non-finite values.
Results may differ from the reference program's by a relative error of at most 0.012.
The reference program's roundings to bfloat16 on the way count: a program that leaves them out, or rounds other values in their place, can miss the bound.
Values may be sent and summed in bfloat16 or wider, within the bound.
No kernel may reach another device: no remote copies, remote signals or barrier semaphores. Data moves between devices by JAX's collectives and lax.ppermute only.
A program may use at most 128 MiB of HBM per device.

```python
import jax
import jax.numpy as jnp
from jax import lax

D = 4608
QH = 16
KVH = 8
HD = 128
WIN = 4096
PAGE = 128
TOK_DEV = 512
STREAM = 32768
PAGES_DEV = 4
NPAGES = 256
SEGS = 16
N_SEQ = 64


def draw_hidden(key, part):
    key_base, key_cols, key_rows = jax.random.split(key, 3)
    columns = jnp.arange(D, dtype=jnp.float32)
    rising = jnp.exp(jnp.log(3.0) * columns / D) * jax.random.uniform(key_cols, (D,), jnp.float32, 0.7, 1.4)
    row_scales = jnp.exp(jax.random.uniform(key_rows, (STREAM, 1), jnp.float32, 0.0, jnp.log(10.0)))
    base = jnp.clip(jax.random.normal(key_base, (STREAM, D), jnp.float32), -4.0, 4.0)
    return (base * row_scales * rising[None, :] * 0.25).astype(jnp.bfloat16)


def draw_segment_ids(key, part):
    key_offsets, key_middle = jax.random.split(jax.random.fold_in(key, 7), 2)
    half_win = WIN // 2
    base_points = jnp.arange(1, SEGS, dtype=jnp.int32) * half_win
    offsets = jax.random.randint(key_offsets, (SEGS - 1,), 1, half_win, dtype=jnp.int32)
    middle_offset = jax.random.randint(key_middle, (), 1, min(TOK_DEV, half_win), dtype=jnp.int32)
    offsets = offsets.at[SEGS // 2 - 1].set(middle_offset)
    bounds = base_points + offsets
    bounds = jnp.where(bounds % TOK_DEV == 0, bounds + 1, bounds)
    token_index = jnp.arange(STREAM, dtype=jnp.int32)
    return jnp.sum((token_index[:, None] >= bounds[None, :]).astype(jnp.int32), axis=1).astype(jnp.int32)


def level_of(key, shape, cuts, low, high):
    gain = 1.0
    for axis_at, blocks in cuts:
        draws = jax.random.uniform(jax.random.fold_in(jax.random.fold_in(key, 6), axis_at), (blocks,), jnp.float32, low / len(cuts), high / len(cuts))
        gain = gain * jnp.repeat(jnp.exp(draws), shape[axis_at] // blocks).reshape((-1,) + (1,) * (len(shape) - 1 - axis_at))
    return gain


def gaussian(key, dims, deviation, reach, pieces=(), kind=jnp.bfloat16):
    array = jax.random.normal(key, dims, jnp.float32) * deviation
    if len(pieces) > 0:
        array = level_of(key, dims, pieces, -0.22, 0.18) * array
    return jnp.clip(array, min=-reach, max=reach).astype(kind)


def setup_inputs(seed: int = 0) -> dict:
    streams_of = jax.random.split(jax.random.key(seed), 8)
    return {
        "hidden": draw_hidden(jax.random.fold_in(streams_of[7], 71), 0),
        "norm_gain": jnp.clip(1.0 + 0.18 * jax.random.normal(streams_of[1], (D,), jnp.float32), 0.1, 1.9),
        "w_query": gaussian(streams_of[2], (D, QH * HD), (D // 7) ** -0.5, 0.25, ((1, 4),)),
        "w_key": gaussian(streams_of[3], (D, KVH * HD), D ** -0.5, 0.09375, ((1, 4),)),
        "w_value": gaussian(streams_of[4], (D, KVH * HD), D ** -0.5, 0.09375, ((1, 4),)),
        "segment_ids": draw_segment_ids(jax.random.fold_in(streams_of[7], 71), 0),
        "page_table": jax.vmap(lambda own: jax.random.permutation(own, PAGES_DEV))(jax.random.split(streams_of[6], N_SEQ)).reshape((N_SEQ, PAGES_DEV)).astype(jnp.int32),
    }


logit_cap = 50.0
query_scale = 144.0 ** (-0.5)
norm_eps = 1e-06

def rotate(heads, positions):
    half_dim = HD // 2
    freqs = 10000.0 ** (-(jnp.arange(half_dim, dtype=jnp.float32) * (2.0 / HD)))
    angles = positions.astype(jnp.float32)[:, None] * freqs[None, :]
    cosine = jnp.cos(angles)[:, None, :]
    sine_part = jnp.sin(angles)[:, None, :]
    first_half = heads[..., :half_dim]
    second_half = heads[..., half_dim:]
    return jnp.concatenate([first_half * cosine - second_half * sine_part, second_half * cosine + first_half * sine_part], axis=-1)

def reference(hidden, norm_gain, w_query, w_key, w_value, segment_ids, page_table):
    wide = hidden.astype(jnp.float32)
    meansq = lax.optimization_barrier(jnp.mean(wide * wide, axis=-1, keepdims=True))
    normed = (wide * lax.rsqrt(meansq + norm_eps) * norm_gain).astype(jnp.bfloat16)
    queries_raw = jnp.dot(normed, w_query, preferred_element_type=jnp.float32)
    keys_raw = jnp.dot(normed, w_key, preferred_element_type=jnp.float32)
    values = jnp.dot(normed, w_value, preferred_element_type=jnp.float32).astype(jnp.bfloat16)
    index_all = jnp.arange(STREAM, dtype=jnp.int32)
    earlier = jnp.concatenate([jnp.full((1,), -1, jnp.int32), segment_ids[:-1].astype(jnp.int32)])
    marks = jnp.where(segment_ids != earlier, index_all, 0).astype(jnp.int32)
    starts = lax.cummax(marks, axis=0)
    positions = index_all - starts
    queries = rotate(queries_raw.reshape(STREAM, QH, HD), positions).astype(jnp.bfloat16)
    queries = queries.reshape(STREAM, KVH, QH // KVH, HD)
    keys = rotate(keys_raw.reshape(STREAM, KVH, HD), positions).astype(jnp.bfloat16)
    value_heads = values.reshape(STREAM, KVH, HD)
    pad_keys = jnp.concatenate([jnp.zeros((WIN, KVH, HD), jnp.bfloat16), keys], axis=0)
    pad_values = jnp.concatenate([jnp.zeros((WIN, KVH, HD), jnp.bfloat16), value_heads], axis=0)

    def one_block(block_id):
        first = (block_id * TOK_DEV).astype(jnp.int32)
        query_block = lax.dynamic_slice_in_dim(queries, first, TOK_DEV, 0).astype(jnp.float32)
        key_block = lax.dynamic_slice_in_dim(pad_keys, first, WIN + TOK_DEV, 0).astype(jnp.float32)
        value_block = lax.dynamic_slice_in_dim(pad_values, first, WIN + TOK_DEV, 0).astype(jnp.float32)
        start_block = lax.dynamic_slice_in_dim(starts, first, TOK_DEV, 0)
        query_index = first + jnp.arange(TOK_DEV, dtype=jnp.int32)
        key_index = first - WIN + jnp.arange(WIN + TOK_DEV, dtype=jnp.int32)
        scores = jnp.einsum('qgrd,kgd->grqk', query_block, key_block) * query_scale
        capped = logit_cap * jnp.tanh(scores / logit_cap)
        allowed = (key_index[None, :] >= start_block[:, None]) & (key_index[None, :] <= query_index[:, None]) & (query_index[:, None] - key_index[None, :] < WIN)
        weights = jnp.where(allowed, jnp.exp(capped), 0.0)
        totals = lax.optimization_barrier(jnp.sum(weights, axis=-1))
        rounded = lax.optimization_barrier(weights.astype(jnp.bfloat16)).astype(jnp.float32)
        numerator = jnp.einsum('grqk,kgd->grqd', rounded, value_block)
        mixed = numerator / totals[..., None]
        return jnp.transpose(mixed, (2, 0, 1, 3)).reshape(TOK_DEV, QH * HD).astype(jnp.bfloat16)
    attended = lax.map(one_block, jnp.arange(STREAM // TOK_DEV, dtype=jnp.int32)).reshape(STREAM, QH * HD)
    stacked = jnp.stack([keys.reshape(STREAM, KVH * HD), values], axis=1).reshape(NPAGES, PAGE, 2, KVH * HD)
    page_ids = jnp.arange(NPAGES, dtype=jnp.int32)
    targets = page_ids // PAGES_DEV * PAGES_DEV + page_table.reshape(NPAGES).astype(jnp.int32)
    kv_cache = jnp.zeros_like(stacked).at[targets].set(stacked)
    return (attended, kv_cache)
```

```python
import functools

import jax
import jax.numpy as jnp
import numpy as np
from jax import lax
from jax.experimental import pallas as pl
from jax.experimental.pallas import tpu as pltpu
from jax.sharding import PartitionSpec as P

HD = 128
WIN = 4096
PAGE = 128
TILE = 256

logit_cap = 50.0
query_scale = 144.0 ** (-0.5)
norm_eps = 1e-06
log2e = 1.4426950408889634

VMEM = pltpu.VMEM
SMEM = pltpu.SMEM


def whole(space=VMEM):
    return pl.BlockSpec(memory_space=space)


def shifted(block, axis, distance):
    devices = range(lax.axis_size(axis))
    route = [(i - distance, i) for i in devices if i - distance in devices]
    return lax.ppermute(block, axis, route)


def turned(block, axis, distance):
    count = lax.axis_size(axis)
    return lax.ppermute(block, axis, [(i, (i + distance) % count) for i in range(count)])


def swapped(block):
    return lax.ppermute(block, "seq", [(i, i ^ 1) for i in range(lax.axis_size("seq"))])


def rope(x, cos, sin):
    return x * cos + pltpu.roll(x, HD // 2, 1) * sin


def kv_kernel(rank_ref, *refs):
    own, left, right, far_a, far_b, gain, wk, wv, cos, sin, normed, kv0, kv1 = refs
    rows, width = own.shape
    features = gain.shape[1]
    half = rows // 2
    rank = rank_ref[0]

    for start in range(0, rows, 128):
        at = pl.ds(start, 128)
        far = far_a[at, :] if start < half else far_b[pl.ds(start - half, 128), :]
        pieces = ((own[at, :], 0), (left[at, :], 3), (right[at, :], 1), (far, 2))
        square = 0.0
        for piece, turn in pieces:
            wide = piece.astype(jnp.float32)
            square = square + jnp.sum(wide * wide, axis=-1, keepdims=True)
        scale = lax.rsqrt(square * (1.0 / features) + norm_eps)
        for piece, turn in pieces:
            shard = lax.rem(rank + turn, 4)
            cols = pl.ds(pl.multiple_of(shard * width, 128), width)
            wide = piece.astype(jnp.float32)
            normed[at, cols] = (wide * scale * gain[:, cols]).astype(jnp.bfloat16)
    keys = jnp.dot(normed[...], wk[...], preferred_element_type=jnp.float32)
    values = jnp.dot(normed[...], wv[...], preferred_element_type=jnp.float32)
    kv_width = wk.shape[1]
    for out, start in ((kv0, 0), (kv1, half)):
        at = slice(start, start + half)
        for head in range(kv_width // HD):
            cols = slice(head * HD, head * HD + HD)
            out[:, cols] = rope(keys[at, cols], cos[at, :], sin[at, :]).astype(jnp.bfloat16)
        out[:, kv_width:] = values[at].astype(jnp.bfloat16)


def project_kv(rank, pieces, gain, wk, wv, cos, sin):
    rows, width = pieces[0].shape
    features = wk.shape[0]
    half = jax.ShapeDtypeStruct((rows // 2, 2 * wk.shape[1]), jnp.bfloat16)
    return pl.pallas_call(
        kv_kernel,
        name="norm_project_kv",
        out_shape=(jax.ShapeDtypeStruct((rows, features), jnp.bfloat16), half, half),
        in_specs=[whole(SMEM)] + [whole()] * 10,
        out_specs=(whole(), whole(), whole()),
        compiler_params=pltpu.CompilerParams(vmem_limit_bytes=40 << 20),
        cost_estimate=pl.CostEstimate(
            flops=2 * rows * features * 2 * wk.shape[1],
            transcendentals=rows,
            bytes_accessed=2 * (2 * rows * features + 2 * features * wk.shape[1]),
        ),
    )(rank, *pieces, gain, wk, wv, cos, sin)


def q_kernel(normed, wq, cos, sin, out):
    raw = jnp.dot(normed[...], wq[...], preferred_element_type=jnp.float32)
    for head in range(wq.shape[1] // HD):
        cols = slice(head * HD, head * HD + HD)
        out[:, cols] = rope(raw[:, cols], cos[...], sin[...]).astype(jnp.bfloat16)


def project_q(normed, wq, cos, sin):
    rows, features = normed.shape
    return pl.pallas_call(
        q_kernel,
        name="project_q",
        out_shape=jax.ShapeDtypeStruct((rows, wq.shape[1]), jnp.bfloat16),
        in_specs=[whole()] * 4,
        out_specs=whole(),
        compiler_params=pltpu.CompilerParams(vmem_limit_bytes=24 << 20),
        cost_estimate=pl.CostEstimate(
            flops=2 * rows * features * wq.shape[1],
            transcendentals=0,
            bytes_accessed=2 * (rows * features + features * wq.shape[1]),
        ),
    )(normed, wq, cos, sin)


def attend_kernel(places, first, last, meta, low_ref, q_ref, *refs):
    count = len(places)
    blocks = refs[:count]
    refs = refs[count:]
    if first:
        acc, tot = refs[-2:]
        acc[...] = jnp.zeros_like(acc)
        tot[...] = jnp.zeros_like(tot)
    else:
        acc_in, tot_in = refs[:2]
        if last:
            out, acc, tot = refs[2:]
        else:
            acc, tot = refs[2:]
        acc[...] = acc_in[...]
        tot[...] = tot_in[...]
    rows = q_ref.shape[0]
    heads = q_ref.shape[1] // HD
    kv_width = blocks[0].shape[1] // 2
    repeat = heads * HD // kv_width
    for block, (distance, offset) in zip(blocks, places):
        span = block.shape[0]
        key_first = meta[0] - distance * rows + offset
        for tile in range(rows // TILE):
            if distance == 0 and offset >= (tile + 1) * TILE:
                continue

            @pl.when(key_first + (span - 1) >= meta[1 + tile])
            def _(block=block, tile=tile):
                at = slice(tile * TILE, tile * TILE + TILE)
                key_index = key_first + lax.broadcasted_iota(jnp.int32, (TILE, span), 1)
                allowed = key_index >= low_ref[at, :]
                if distance == 0 and offset + span > tile * TILE:
                    row = meta[0] + tile * TILE + lax.broadcasted_iota(jnp.int32, (TILE, span), 0)
                    allowed = allowed & (key_index <= row)
                for head in range(heads):
                    cols = slice(head * HD, head * HD + HD)
                    group = head // repeat
                    keys = block[:, group * HD : group * HD + HD]
                    values = block[:, kv_width + group * HD : kv_width + group * HD + HD]
                    raw = lax.dot_general(
                        q_ref[at, cols],
                        keys,
                        (((1,), (1,)), ((), ())),
                        preferred_element_type=jnp.float32,
                    )
                    capped = jnp.tanh(raw * (query_scale / logit_cap))
                    weights = jnp.where(allowed, jnp.exp2(capped * (logit_cap * log2e)), 0.0)
                    part = weights[:, :HD]
                    for k in range(HD, span, HD):
                        part = part + weights[:, k : k + HD]
                    tot[at, cols] += part
                    acc[at, cols] += jnp.dot(
                        weights.astype(jnp.bfloat16), values, preferred_element_type=jnp.float32
                    )
    if last:
        for head in range(heads):
            cols = slice(head * HD, head * HD + HD)
            total = jnp.sum(tot[:, cols], axis=-1, keepdims=True)
            out[:, cols] = (acc[:, cols] / total).astype(jnp.bfloat16)


def attend(meta, low, queries, parts, state=None, last=False):
    rows, width = queries.shape
    places = tuple((distance, offset) for _, distance, offset in parts)
    blocks = [block for block, _, _ in parts]
    wide = jax.ShapeDtypeStruct((rows, width), jnp.float32)
    first = state is None
    operands = [meta, low, queries, *blocks] + ([] if first else list(state))
    keys = sum(block.shape[0] for block in blocks)
    scratch = ()
    aliases = {}
    if last:
        out_shape = jax.ShapeDtypeStruct((rows, width), jnp.bfloat16)
        out_specs = whole()
        scratch = (VMEM((rows, width), jnp.float32), VMEM((rows, width), jnp.float32))
    else:
        out_shape = (wide, wide)
        out_specs = (whole(), whole())
    return pl.pallas_call(
        functools.partial(attend_kernel, places, first, last),
        name="attend_last" if last else "attend",
        out_shape=out_shape,
        in_specs=[whole(SMEM)] + [whole()] * (len(operands) - 1),
        out_specs=out_specs,
        scratch_shapes=scratch,
        input_output_aliases=aliases,
        compiler_params=pltpu.CompilerParams(vmem_limit_bytes=24 << 20),
        cost_estimate=pl.CostEstimate(
            flops=4 * rows * width * keys,
            transcendentals=2 * rows * width // HD * keys,
            bytes_accessed=4 * rows * width,
        ),
    )(*operands)


def per_device(hidden, norm_gain, w_query, w_key, w_value, segment_ids, page_table):
    tokens = hidden.shape[0]
    place = lax.axis_index("seq")
    rank = lax.axis_index("tp")
    half = tokens // 2

    left = turned(hidden, "tp", 1)
    right = turned(hidden, "tp", -1)
    far_a = turned(left[:half], "tp", 1)
    far_b = turned(right[half:], "tp", -1)

    marked = (segment_ids + 1).reshape(1, tokens)
    near = jnp.concatenate(
        [marked, shifted(marked, "seq", 1), shifted(marked, "seq", 2)], axis=0
    )
    earlier = jnp.concatenate(
        [near[1:], shifted(near, "seq", 3), shifted(near, "seq", 6)], axis=0
    ).reshape(1, -1)
    first_token = place * tokens
    own = segment_ids.reshape(tokens, 1) + 1
    before = jnp.sum((marked < own).astype(jnp.int32), axis=1, keepdims=True)
    same = jnp.sum((earlier == own).astype(jnp.int32), axis=1, keepdims=True)
    starts = first_token + before - same
    query_index = first_token + jnp.arange(tokens, dtype=jnp.int32)[:, None]
    low = jnp.maximum(starts, query_index - (WIN - 1))
    meta = jnp.concatenate([first_token.reshape(1), low[::TILE, 0]])

    freqs = 10000.0 ** (-(jnp.arange(HD // 2, dtype=jnp.float32) * (2.0 / HD)))
    angles = (query_index - starts).astype(jnp.float32) * jnp.concatenate([freqs, freqs])[None, :]
    sign = np.where(np.arange(HD) < HD // 2, -1.0, 1.0).astype(np.float32)
    cos = jnp.cos(angles)
    sin = jnp.sin(angles) * sign[None, :]

    normed, *streams = project_kv(
        rank.reshape(1),
        (hidden, left, right, far_a, far_b),
        norm_gain.reshape(1, -1),
        w_key,
        w_value,
        cos,
        sin,
    )
    queries = project_q(normed, w_query, cos, sin)

    kv_width = w_key.shape[1]
    pages_here = tokens // PAGE
    slot_ids = jnp.arange(pages_here, dtype=jnp.int32)
    table = page_table[0]
    source = jnp.sum(jnp.where(table[None, :] == slot_ids[:, None], slot_ids[None, :], 0), axis=1)
    pages = jnp.concatenate(streams, axis=0).reshape(pages_here, PAGE, 2 * kv_width)
    ordered = jnp.take(pages, source, axis=0)
    received = lax.all_to_all(ordered, "tp", split_axis=0, concat_axis=0, tiled=True)
    kv_cache = (
        received.reshape(-1, PAGE, 2, kv_width).transpose(1, 2, 0, 3).reshape(1, PAGE, 2, -1)
    )

    offsets = [s * half for s in range(len(streams))]
    state = attend(meta, low, queries, [(b, 0, o) for b, o in zip(streams, offsets)])
    odd = place % 2 == 1
    steps = WIN // tokens // 2
    current = streams
    for step in range(1, steps + 1):
        arrived = [shifted(block, "seq", 2) for block in current]
        crossed = [swapped(jnp.where(odd, new, old)) for new, old in zip(arrived, current)]
        current = arrived
        groups = [
            [(a, 2 * step, o), (c, 2 * step - 1, o)] for a, c, o in zip(arrived, crossed, offsets)
        ]
        if step < steps:
            state = attend(meta, low, queries, groups[0] + groups[1], state)
        else:
            state = attend(meta, low, queries, groups[0], state)
            attended = attend(meta, low, queries, groups[1], state, last=True)
    return (attended, kv_cache)


def solution(mesh):
    placed = (
        P("seq", "tp"),
        P(),
        P(None, "tp"),
        P(None, "tp"),
        P(None, "tp"),
        P("seq"),
        P("seq", None),
    )
    return jax.shard_map(
        per_device,
        mesh=mesh,
        in_specs=placed,
        out_specs=(P("seq", "tp"), P(("seq", "tp"), None, None, None)),
        check_vma=False,
    )
```

```python
import functools

import jax
import jax.numpy as jnp
import numpy as np
from jax import lax
from jax.experimental import pallas as pl
from jax.experimental.pallas import tpu as pltpu
from jax.sharding import PartitionSpec as P

HD = 128
WIN = 4096
PAGE = 128

logit_cap = 50.0
query_scale = 144.0 ** (-0.5)
norm_eps = 1e-06
log2e = 1.4426950408889634

VMEM = pltpu.VMEM
SMEM = pltpu.SMEM


def whole(space=VMEM):
    return pl.BlockSpec(memory_space=space)


def shifted(block, axis, distance):
    devices = range(lax.axis_size(axis))
    route = [(i - distance, i) for i in devices if i - distance in devices]
    return lax.ppermute(block, axis, route)


def turned(block, axis, distance):
    count = lax.axis_size(axis)
    return lax.ppermute(block, axis, [(i, (i + distance) % count) for i in range(count)])


def swapped(block):
    return lax.ppermute(block, "seq", [(i, i ^ 1) for i in range(lax.axis_size("seq"))])


def rope(x, cos, sin):
    return x * cos + pltpu.roll(x, HD // 2, 1) * sin


def kv_kernel(layout, shards, table, *refs):
    segments, first_page, carried, count = layout
    pieces = refs[: len(segments)]
    gain, wk, wv, cos, sin = refs[len(segments) : len(segments) + 5]
    outs = refs[len(segments) + 5 + carried :]
    normed, pages, streams = outs[0], outs[1], outs[2:]
    rows = normed.shape[0]
    features = gain.shape[1]
    width = features // count

    for start in range(0, rows, 128):
        at = pl.ds(start, 128)
        blocks = []
        for ref, (turn, begin, end) in zip(pieces, segments):
            if begin <= start < end:
                part = ref.at[turn] if len(ref.shape) == 3 else ref
                blocks.append((part, pl.ds(start - begin, 128), turn))
        square = 0.0
        for part, rows_at, turn in blocks:
            wide = part[rows_at, :].astype(jnp.float32)
            square = square + jnp.sum(wide * wide, axis=-1, keepdims=True)
        scale = lax.rsqrt(square * (1.0 / features) + norm_eps)
        for part, rows_at, turn in blocks:
            cols = pl.ds(pl.multiple_of(shards[turn] * width, 128), width)
            wide = part[rows_at, :].astype(jnp.float32)
            normed[at, cols] = (wide * scale * gain[:, cols]).astype(jnp.bfloat16)
    keys = jnp.dot(normed[...], wk[...], preferred_element_type=jnp.float32)
    values = jnp.dot(normed[...], wv[...], preferred_element_type=jnp.float32)
    kv_width = wk.shape[1]
    size = streams[0].shape[0]
    for start in range(0, rows, PAGE):
        at = slice(start, start + PAGE)
        slot = table[first_page + start // PAGE]
        out = streams[start // size]
        to = slice(start % size, start % size + PAGE)
        for head in range(kv_width // HD):
            cols = slice(head * HD, head * HD + HD)
            turned_keys = rope(keys[at, cols], cos[at, :], sin[at, :]).astype(jnp.bfloat16)
            out[to, cols] = turned_keys
            pages[slot, :, cols] = turned_keys
        rounded = values[at].astype(jnp.bfloat16)
        out[to, kv_width:] = rounded
        pages[slot, :, kv_width:] = rounded


def project_kv(shards, table, pieces, gain, wk, wv, cos, sin, size, first_page=0, pages=None):
    features = wk.shape[0]
    rows = cos.shape[0]
    width = 2 * wk.shape[1]
    segments = tuple(where for _, where in pieces)
    arrays = []
    for array, _ in pieces:
        arrays.append(array)
    carried = pages is not None
    operands = [shards, table, *arrays, gain, wk, wv, cos, sin] + ([pages] if carried else [])
    stream = jax.ShapeDtypeStruct((size, width), jnp.bfloat16)
    paged = jax.ShapeDtypeStruct((table.shape[0], PAGE, width), jnp.bfloat16)
    out_shape = (jax.ShapeDtypeStruct((rows, features), jnp.bfloat16), paged)
    out_shape = out_shape + (stream,) * (rows // size)
    specs = [whole(SMEM)] * 2 + [whole()] * (len(operands) - 2)
    return pl.pallas_call(
        functools.partial(kv_kernel, (segments, first_page, carried, shards.shape[0])),
        name="norm_project_kv",
        out_shape=out_shape,
        in_specs=specs,
        out_specs=(whole(),) * len(out_shape),
        input_output_aliases={len(operands) - 1: 1} if carried else {},
        compiler_params=pltpu.CompilerParams(vmem_limit_bytes=14 << 20),
        cost_estimate=pl.CostEstimate(
            flops=2 * rows * features * width,
            transcendentals=rows,
            bytes_accessed=2 * (2 * rows * features + features * width),
        ),
    )(*operands)


def q_kernel(count, *refs):
    normed = refs[:count]
    wq, cos, sin, out = refs[count:]
    start = 0
    for block in normed:
        at = slice(start, start + block.shape[0])
        raw = jnp.dot(block[...], wq[...], preferred_element_type=jnp.float32)
        for head in range(wq.shape[1] // HD):
            cols = slice(head * HD, head * HD + HD)
            out[at, cols] = rope(raw[:, cols], cos[at, :], sin[at, :]).astype(jnp.bfloat16)
        start += block.shape[0]


def project_q(normed, wq, cos, sin):
    rows = cos.shape[0]
    features, width = wq.shape
    return pl.pallas_call(
        functools.partial(q_kernel, len(normed)),
        name="project_q",
        out_shape=jax.ShapeDtypeStruct((rows, width), jnp.bfloat16),
        in_specs=[whole()] * (len(normed) + 3),
        out_specs=whole(),
        compiler_params=pltpu.CompilerParams(vmem_limit_bytes=10 << 20),
        cost_estimate=pl.CostEstimate(
            flops=10000000 * rows,
            transcendentals=0,
            bytes_accessed=rows * width,
        ),
    )(*normed, wq, cos, sin)


def attend_kernel(places, first, last, guarded, meta, low_ref, q_ref, *refs):
    count = len(places)
    blocks = refs[:count]
    refs = refs[count:]
    if first:
        acc, tot = refs[-2:]
        acc[...] = jnp.zeros_like(acc)
        tot[...] = jnp.zeros_like(tot)
    else:
        acc_in, tot_in = refs[:2]
        if last:
            out, acc, tot = refs[2:]
            acc[...] = acc_in[...]
            tot[...] = tot_in[...]
        else:
            acc, tot = refs[2:]
    rows = q_ref.shape[0]
    heads = q_ref.shape[1] // HD
    kv_width = blocks[0].shape[1] // 2
    repeat = heads * HD // kv_width

    def visit(block, index, top):
        span = block.shape[0]
        key_first = meta[index]
        at = slice(top or 0, rows)
        here = (at.stop - at.start, span)
        key_index = key_first + lax.broadcasted_iota(jnp.int32, here, 1)
        allowed = key_index >= low_ref[at, :]
        if top is not None:
            row = meta[0] + top + lax.broadcasted_iota(jnp.int32, here, 0)
            allowed = allowed & (key_index <= row)
        for head in range(heads):
            cols = slice(head * HD, head * HD + HD)
            group = head // repeat
            keys = block[:, group * HD : group * HD + HD]
            values = block[:, kv_width + group * HD : kv_width + group * HD + HD]
            raw = lax.dot_general(
                q_ref[at, cols],
                keys,
                (((1,), (1,)), ((), ())),
                preferred_element_type=jnp.float32,
            )
            capped = jnp.tanh(raw * (query_scale / logit_cap))
            weights = jnp.where(allowed, jnp.exp2(capped * (logit_cap * log2e)), 0.0)
            part = weights[:, :HD]
            for k in range(HD, span, HD):
                part = part + weights[:, k : k + HD]
            tot[at, cols] += part
            acc[at, cols] += jnp.dot(
                weights.astype(jnp.bfloat16), values, preferred_element_type=jnp.float32
            )

    def visit_all():
        for block, (index, top) in zip(blocks, places):
            visit(block, index, top)

    if guarded:
        key_first = meta[places[0][0]]
        pl.when((key_first <= meta[0]) & (key_first + rows > meta[0] - WIN))(visit_all)
    else:
        visit_all()
    if last:
        for head in range(heads):
            cols = slice(head * HD, head * HD + HD)
            total = jnp.sum(tot[:, cols], axis=-1, keepdims=True)
            out[:, cols] = (acc[:, cols] / total).astype(jnp.bfloat16)


def attend(meta, low, queries, parts, state=None, last=False, guarded=False):
    rows, width = queries.shape
    places = tuple((index, top) for _, index, top in parts)
    blocks = [block for block, _, _ in parts]
    wide = jax.ShapeDtypeStruct((rows, width), jnp.float32)
    first = state is None
    operands = [meta, low, queries, *blocks] + ([] if first else list(state))
    keys = sum(block.shape[0] for block in blocks)
    scratch = ()
    aliases = {}
    if last:
        out_shape = jax.ShapeDtypeStruct((rows, width), jnp.bfloat16)
        out_specs = whole()
        scratch = (VMEM((rows, width), jnp.float32), VMEM((rows, width), jnp.float32))
    else:
        out_shape = (wide, wide)
        out_specs = (whole(), whole())
        if not first:
            aliases = {len(operands) - 2: 0, len(operands) - 1: 1}
    return pl.pallas_call(
        functools.partial(attend_kernel, places, first, last, guarded),
        name="attend_last" if last else "attend",
        out_shape=out_shape,
        in_specs=[whole(SMEM)] + [whole()] * (len(operands) - 1),
        out_specs=out_specs,
        scratch_shapes=scratch,
        input_output_aliases=aliases,
        compiler_params=pltpu.CompilerParams(vmem_limit_bytes=8 << 20),
        cost_estimate=pl.CostEstimate(
            flops=10000000 * keys,
            transcendentals=0,
            bytes_accessed=width * keys,
        ),
    )(*operands)


def cache_kernel(received, out):
    width = received.shape[2] // 2
    for shard in range(received.shape[0]):
        cols = slice(shard * width, shard * width + width)
        for index in range(2):
            block = received[shard, :, index * width : index * width + width]
            out[0, :, index, cols] = block


def build_cache(received):
    ranks, rows, width = received.shape
    return pl.pallas_call(
        cache_kernel,
        name="build_cache",
        out_shape=jax.ShapeDtypeStruct((1, rows, 2, ranks * width // 2), received.dtype),
        in_specs=[whole()],
        out_specs=whole(),
        compiler_params=pltpu.CompilerParams(vmem_limit_bytes=8 << 20),
    )(received)


def after(value, *others):
    return lax.optimization_barrier((value, *others))[0]


def ring_gather(block):
    rows = block.shape[0]
    half = rows // 2
    left = turned(block, "tp", 1)
    right = turned(block, "tp", -1)
    far_a = turned(left[:half], "tp", 1)
    far_b = turned(right[half:], "tp", -1)
    return [
        (block, (0, 0, rows)),
        (left, (3, 0, rows)),
        (right, (1, 0, rows)),
        (far_a, (2, 0, half)),
        (far_b, (2, half, rows)),
    ]


def per_device(hidden, norm_gain, w_query, w_key, w_value, segment_ids, page_table):
    tokens = hidden.shape[0]
    place = lax.axis_index("seq")
    rank = lax.axis_index("tp")
    half = tokens // 2
    ranks = lax.axis_size("tp")
    shards = (rank + jnp.arange(ranks, dtype=jnp.int32)) % ranks
    table = page_table[0]

    pieces = ring_gather(hidden)
    marked = (segment_ids + 1).reshape(1, tokens)
    near = jnp.concatenate(
        [marked, shifted(marked, "seq", 1), shifted(marked, "seq", 2)], axis=0
    )
    earlier = jnp.concatenate(
        [near[1:], shifted(near, "seq", 3), shifted(near, "seq", 6)], axis=0
    ).reshape(1, -1)
    first_token = place * tokens
    own = segment_ids.reshape(tokens, 1) + 1
    before = jnp.sum((marked < own).astype(jnp.int32), axis=1, keepdims=True)
    same = jnp.sum((earlier == own).astype(jnp.int32), axis=1, keepdims=True)
    starts = first_token + before - same
    query_index = first_token + jnp.arange(tokens, dtype=jnp.int32)[:, None]
    low = jnp.maximum(starts, query_index - (WIN - 1))
    steps = WIN // tokens // 2
    core = place % 2
    backs = [jnp.int32(2 * step) for step in range(steps + 1)]
    backs += [2 * step - 1 + 2 * core for step in range(steps + 1)]
    firsts = jnp.stack(backs) * -tokens + first_token
    meta = jnp.concatenate([first_token.reshape(1), firsts, firsts + half])

    freqs = 10000.0 ** (-(jnp.arange(HD // 2, dtype=jnp.float32) * (2.0 / HD)))
    angles = (query_index - starts).astype(jnp.float32) * jnp.concatenate([freqs, freqs])[None, :]
    sign = np.where(np.arange(HD) < HD // 2, -1.0, 1.0).astype(np.float32)
    cos = jnp.cos(angles)
    sin = jnp.sin(angles) * sign[None, :]
    gain = norm_gain.reshape(1, -1)

    normed, pages, a0, b0 = project_kv(
        shards, table, pieces, gain, w_key, w_value, cos, sin, half
    )

    def hop(name, block):
        with jax.named_scope(name):
            return shifted(block, "seq", 2)

    def cross(name, block):
        with jax.named_scope(name):
            return swapped(block)

    look = functools.partial(attend, meta, low)
    straight = [1 + step for step in range(steps + 1)]
    turned_at = [2 + steps + step for step in range(steps + 1)]
    later = 2 * (steps + 1)

    a, b = [a0], [b0]
    ca, cb = [], []
    for step in range(steps + 1):
        if step:
            a.append(hop(f"hop_a{step}", a[-1]))
            b.append(hop(f"hop_b{step}", b[-1]))
        ca.append(cross(f"cross_a{step}", a[-1]))
        cb.append(cross(f"cross_b{step}", b[-1]))
    queries = project_q((normed,), w_query, cos, sin)
    state = look(queries, [(a[0], straight[0], 0), (b[0], straight[0] + later, half)])
    edge = [(ca[0], turned_at[0], None), (cb[0], turned_at[0] + later, None)]
    state = look(queries, edge, state, guarded=True)
    for step in range(1, steps):
        near, over = straight[step], turned_at[step]
        state = look(queries, [(a[step], near, None), (ca[step], over, None)], state)
        near, over = near + later, over + later
        state = look(queries, [(b[step], near, None), (cb[step], over, None)], state)
    near, over = straight[steps], turned_at[steps]
    state = look(queries, [(a[steps], near, None), (b[steps], near + later, None)], state)
    edge = [(ca[steps], over, None), (cb[steps], over + later, None)]
    attended = look(queries, edge, state, last=True, guarded=True)
    received = lax.all_to_all(after(pages, a[1]), "tp", split_axis=0, concat_axis=0, tiled=True)
    kv_cache = build_cache(received)
    return (attended, kv_cache)


def solution(mesh):
    placed = (
        P("seq", "tp"),
        P(),
        P(None, "tp"),
        P(None, "tp"),
        P(None, "tp"),
        P("seq"),
        P("seq", None),
    )
    return jax.shard_map(
        per_device,
        mesh=mesh,
        in_specs=placed,
        out_specs=(P("seq", "tp"), P(("seq", "tp"), None, None, None)),
        check_vma=False,
    )
```

```python
import functools

import jax
import jax.numpy as jnp
import numpy as np
from jax import lax
from jax.experimental import pallas as pl
from jax.experimental.pallas import tpu as pltpu
from jax.sharding import PartitionSpec as P

HD = 128
WIN = 4096
PAGE = 128
SPAN = 256

logit_cap = 50.0
query_scale = 144.0 ** (-0.5)
norm_eps = 1e-06
log2e = 1.4426950408889634

VMEM = pltpu.VMEM
SMEM = pltpu.SMEM


def whole(space=VMEM):
    return pl.BlockSpec(memory_space=space)


def shifted(block, axis, distance):
    devices = range(lax.axis_size(axis))
    route = [(i - distance, i) for i in devices if i - distance in devices]
    return lax.ppermute(block, axis, route)


def turned(block, axis, distance):
    count = lax.axis_size(axis)
    return lax.ppermute(block, axis, [(i, (i + distance) % count) for i in range(count)])


def swapped(block):
    return lax.ppermute(block, "seq", [(i, i ^ 1) for i in range(lax.axis_size("seq"))])


def rope(x, cos, sin):
    return x * cos + pltpu.roll(x, HD // 2, 1) * sin


def kv_kernel(layout, shards, table, *refs):
    segments, first_page, carried, count = layout
    pieces = refs[: len(segments)]
    gain, wk, wv, cos, sin = refs[len(segments) : len(segments) + 5]
    outs = refs[len(segments) + 5 + carried :]
    normed, pages, streams = outs[0], outs[1], outs[2:]
    rows = normed.shape[0]
    features = gain.shape[1]
    width = features // count

    for start in range(0, rows, 128):
        at = pl.ds(start, 128)
        blocks = []
        for ref, (turn, begin, end) in zip(pieces, segments):
            if begin <= start < end:
                part = ref.at[turn] if len(ref.shape) == 3 else ref
                blocks.append((part, pl.ds(start - begin, 128), turn))
        square = 0.0
        for part, rows_at, turn in blocks:
            wide = part[rows_at, :].astype(jnp.float32)
            square = square + jnp.sum(wide * wide, axis=-1, keepdims=True)
        scale = lax.rsqrt(square * (1.0 / features) + norm_eps)
        for part, rows_at, turn in blocks:
            cols = pl.ds(pl.multiple_of(shards[turn] * width, 128), width)
            wide = part[rows_at, :].astype(jnp.float32)
            normed[at, cols] = (wide * scale * gain[:, cols]).astype(jnp.bfloat16)
    keys = jnp.dot(normed[...], wk[...], preferred_element_type=jnp.float32)
    values = jnp.dot(normed[...], wv[...], preferred_element_type=jnp.float32)
    kv_width = wk.shape[1]
    size = streams[0].shape[0]
    for start in range(0, rows, PAGE):
        at = slice(start, start + PAGE)
        slot = lax.rem(table[first_page + start // PAGE] - shards[0] + count, count)
        out = streams[start // size]
        to = slice(start % size, start % size + PAGE)
        for head in range(kv_width // HD):
            cols = slice(head * HD, head * HD + HD)
            turned_keys = rope(keys[at, cols], cos[at, :], sin[at, :]).astype(jnp.bfloat16)
            out[to, cols] = turned_keys
            pages[slot, :, cols] = turned_keys
        rounded = values[at].astype(jnp.bfloat16)
        out[to, kv_width:] = rounded
        pages[slot, :, kv_width:] = rounded


def project_kv(shards, table, pieces, gain, wk, wv, cos, sin, size, first_page=0, pages=None):
    features = wk.shape[0]
    rows = cos.shape[0]
    width = 2 * wk.shape[1]
    segments = tuple(where for _, where in pieces)
    arrays = []
    for array, _ in pieces:
        arrays.append(array)
    carried = pages is not None
    operands = [shards, table, *arrays, gain, wk, wv, cos, sin] + ([pages] if carried else [])
    stream = jax.ShapeDtypeStruct((size, width), jnp.bfloat16)
    paged = jax.ShapeDtypeStruct((table.shape[0], PAGE, width), jnp.bfloat16)
    out_shape = (jax.ShapeDtypeStruct((rows, features), jnp.bfloat16), paged)
    out_shape = out_shape + (stream,) * (rows // size)
    specs = [whole(SMEM)] * 2 + [whole()] * (len(operands) - 2)
    return pl.pallas_call(
        functools.partial(kv_kernel, (segments, first_page, carried, shards.shape[0])),
        name="norm_project_kv",
        out_shape=out_shape,
        in_specs=specs,
        out_specs=(whole(),) * len(out_shape),
        input_output_aliases={len(operands) - 1: 1} if carried else {},
        compiler_params=pltpu.CompilerParams(vmem_limit_bytes=14 << 20),
        cost_estimate=pl.CostEstimate(
            flops=2 * rows * features * width,
            transcendentals=rows,
            bytes_accessed=2 * (2 * rows * features + features * width),
        ),
    )(*operands)


def q_kernel(count, *refs):
    normed = refs[:count]
    wq, cos, sin, out = refs[count:]
    start = 0
    for block in normed:
        at = slice(start, start + block.shape[0])
        raw = jnp.dot(block[...], wq[...], preferred_element_type=jnp.float32)
        for head in range(wq.shape[1] // HD):
            cols = slice(head * HD, head * HD + HD)
            out[at, cols] = rope(raw[:, cols], cos[at, :], sin[at, :]).astype(jnp.bfloat16)
        start += block.shape[0]


def project_q(normed, wq, cos, sin):
    rows = cos.shape[0]
    features, width = wq.shape
    return pl.pallas_call(
        functools.partial(q_kernel, len(normed)),
        name="project_q",
        out_shape=jax.ShapeDtypeStruct((rows, width), jnp.bfloat16),
        in_specs=[whole()] * (len(normed) + 3),
        out_specs=whole(),
        compiler_params=pltpu.CompilerParams(vmem_limit_bytes=10 << 20),
        cost_estimate=pl.CostEstimate(
            flops=10000000 * rows,
            transcendentals=0,
            bytes_accessed=rows * width,
        ),
    )(*normed, wq, cos, sin)


def attend_kernel(places, first, last, guarded, meta, low_ref, q_ref, *refs):
    count = len(places)
    blocks = refs[:count]
    refs = refs[count:]
    if first:
        acc, tot = refs[-2:]
        acc[...] = jnp.zeros_like(acc)
        tot[...] = jnp.zeros_like(tot)
    else:
        acc_in, tot_in = refs[:2]
        if last:
            out, acc, tot = refs[2:]
            acc[...] = acc_in[...]
            tot[...] = tot_in[...]
        else:
            acc, tot = refs[2:]
    rows = q_ref.shape[0]
    heads = q_ref.shape[1] // HD
    kv_width = blocks[0].shape[1] // 2
    repeat = heads * HD // kv_width

    def visit(block, index, base, top):
        span = SPAN
        key_first = meta[index] + base
        at = slice(top or 0, rows)
        here = (at.stop - at.start, span)
        key_index = key_first + lax.broadcasted_iota(jnp.int32, here, 1)
        allowed = key_index >= jnp.concatenate([low_ref[at, :]] * (span // HD), axis=1)
        if top is not None:
            row = meta[0] + top + lax.broadcasted_iota(jnp.int32, here, 0)
            allowed = allowed & (key_index <= row)
        for head in range(heads):
            cols = slice(head * HD, head * HD + HD)
            group = head // repeat
            keys = block[base : base + span, group * HD : group * HD + HD]
            values = block[
                base : base + span, kv_width + group * HD : kv_width + group * HD + HD
            ]
            raw = lax.dot_general(
                q_ref[at, cols],
                keys,
                (((1,), (1,)), ((), ())),
                preferred_element_type=jnp.float32,
            )
            capped = jnp.tanh(raw * (query_scale / logit_cap))
            weights = jnp.where(allowed, jnp.exp2(capped * (logit_cap * log2e)), 0.0)
            part = weights[:, :HD]
            for k in range(HD, span, HD):
                part = part + weights[:, k : k + HD]
            tot[at, cols] += part
            acc[at, cols] += jnp.dot(
                weights.astype(jnp.bfloat16), values, preferred_element_type=jnp.float32
            )

    def visit_all():
        for block, (index, top) in zip(blocks, places):
            for base in range(0, block.shape[0], SPAN):
                visit(block, index, base, None if top is None else top + base)

    if guarded:
        key_first = meta[places[0][0]]
        pl.when((key_first <= meta[0]) & (key_first + rows > meta[0] - WIN))(visit_all)
    else:
        visit_all()
    if last:
        for head in range(heads):
            cols = slice(head * HD, head * HD + HD)
            total = jnp.sum(tot[:, cols], axis=-1, keepdims=True)
            out[:, cols] = (acc[:, cols] / total).astype(jnp.bfloat16)


def attend(meta, low, queries, parts, state=None, last=False, guarded=False):
    rows, width = queries.shape
    places = tuple((index, top) for _, index, top in parts)
    blocks = [block for block, _, _ in parts]
    wide = jax.ShapeDtypeStruct((rows, width), jnp.float32)
    first = state is None
    operands = [meta, low, queries, *blocks] + ([] if first else list(state))
    keys = sum(block.shape[0] for block in blocks)
    scratch = ()
    aliases = {}
    if last:
        out_shape = jax.ShapeDtypeStruct((rows, width), jnp.bfloat16)
        out_specs = whole()
        scratch = (VMEM((rows, width), jnp.float32), VMEM((rows, width), jnp.float32))
    else:
        out_shape = (wide, wide)
        out_specs = (whole(), whole())
        if not first:
            aliases = {len(operands) - 2: 0, len(operands) - 1: 1}
    return pl.pallas_call(
        functools.partial(attend_kernel, places, first, last, guarded),
        name="attend_last" if last else "attend",
        out_shape=out_shape,
        in_specs=[whole(SMEM)] + [whole()] * (len(operands) - 1),
        out_specs=out_specs,
        scratch_shapes=scratch,
        input_output_aliases=aliases,
        compiler_params=pltpu.CompilerParams(vmem_limit_bytes=8 << 20),
        cost_estimate=pl.CostEstimate(
            flops=10000000 * keys,
            transcendentals=0,
            bytes_accessed=width * keys,
        ),
    )(*operands)


def cache_kernel(shards, *refs):
    out = refs[-1]
    count = len(refs) - 1
    width = refs[0].shape[1] // 2
    for turn, received in enumerate(refs[:-1]):
        shard = shards[(count - turn) % count]
        cols = pl.ds(pl.multiple_of(shard * width, 128), width)
        for index in range(2):
            out[0, :, index, cols] = received[:, index * width : index * width + width]


def exchange_pages(shards, pages):
    count, rows, width = pages.shape
    received = [pages[0]]
    for turn in range(1, count):
        received.append(turned(pages[turn], "tp", turn))
    return pl.pallas_call(
        cache_kernel,
        name="build_cache",
        out_shape=jax.ShapeDtypeStruct((1, rows, 2, count * width // 2), pages.dtype),
        in_specs=[whole(SMEM)] + [whole()] * count,
        out_specs=whole(),
        compiler_params=pltpu.CompilerParams(vmem_limit_bytes=8 << 20),
        cost_estimate=pl.CostEstimate(flops=1000000000, transcendentals=0, bytes_accessed=1000),
    )(shards, *received)


def halves_kernel(left, right, left_out, right_out):
    half = left_out.shape[0]
    left_out[...] = left[:half, :]
    right_out[...] = right[half:, :]


def halves(left, right):
    rows, width = left.shape
    half = jax.ShapeDtypeStruct((rows // 2, width), left.dtype)
    return pl.pallas_call(
        halves_kernel,
        name="halves",
        out_shape=(half, half),
        in_specs=[whole()] * 2,
        out_specs=(whole(), whole()),
        compiler_params=pltpu.CompilerParams(vmem_limit_bytes=8 << 20),
        cost_estimate=pl.CostEstimate(flops=20000000000, transcendentals=0, bytes_accessed=4 * rows * width),
    )(left, right)


def ring_gather(block):
    rows = block.shape[0]
    half = rows // 2
    left = turned(block, "tp", 1)
    right = turned(block, "tp", -1)
    left_half, right_half = halves(left, right)
    far_a = turned(left_half, "tp", 1)
    far_b = turned(right_half, "tp", -1)
    return [
        (block, (0, 0, rows)),
        (left, (3, 0, rows)),
        (right, (1, 0, rows)),
        (far_a, (2, 0, half)),
        (far_b, (2, half, rows)),
    ]


def per_device(hidden, norm_gain, w_query, w_key, w_value, segment_ids, page_table):
    tokens = hidden.shape[0]
    place = lax.axis_index("seq")
    rank = lax.axis_index("tp")
    half = tokens // 2
    ranks = lax.axis_size("tp")
    shards = (rank + jnp.arange(ranks, dtype=jnp.int32)) % ranks
    table = page_table[0]

    pieces = ring_gather(hidden)
    marked = (segment_ids + 1).reshape(1, tokens)
    near = jnp.concatenate(
        [marked, shifted(marked, "seq", 1), shifted(marked, "seq", 2)], axis=0
    )
    earlier = jnp.concatenate(
        [near[1:], shifted(near, "seq", 3), shifted(near, "seq", 6)], axis=0
    ).reshape(1, -1)
    first_token = place * tokens
    own = segment_ids.reshape(tokens, 1) + 1
    before = jnp.sum((marked < own).astype(jnp.int32), axis=1, keepdims=True)
    same = jnp.sum((earlier == own).astype(jnp.int32), axis=1, keepdims=True)
    starts = first_token + before - same
    query_index = first_token + jnp.arange(tokens, dtype=jnp.int32)[:, None]
    low = jnp.maximum(starts, query_index - (WIN - 1)) + jnp.zeros((1, HD), jnp.int32)
    steps = WIN // tokens // 2
    core = place % 2
    backs = [jnp.int32(2 * step) for step in range(steps + 1)]
    backs += [2 * step - 1 + 2 * core for step in range(steps + 1)]
    firsts = jnp.stack(backs) * -tokens + first_token
    meta = jnp.concatenate([first_token.reshape(1), firsts])

    freqs = 10000.0 ** (-(jnp.arange(HD // 2, dtype=jnp.float32) * (2.0 / HD)))
    angles = (query_index - starts).astype(jnp.float32) * jnp.concatenate([freqs, freqs])[None, :]
    sign = np.where(np.arange(HD) < HD // 2, -1.0, 1.0).astype(np.float32)
    cos = jnp.cos(angles)
    sin = jnp.sin(angles) * sign[None, :]
    gain = norm_gain.reshape(1, -1)

    normed, pages, stream = project_kv(
        shards, table, pieces, gain, w_key, w_value, cos, sin, tokens
    )
    look = functools.partial(attend, meta, low)
    arrived = [stream]
    crossed = []
    for step in range(steps + 1):
        if step:
            with jax.named_scope(f"hop_{step}"):
                arrived.append(shifted(arrived[-1], "seq", 2))
        with jax.named_scope(f"cross_{step}"):
            crossed.append(swapped(arrived[-1]))
    straight = [1 + step for step in range(steps + 1)]
    over = [2 + steps + step for step in range(steps + 1)]
    queries = project_q((normed,), w_query, cos, sin)
    state = look(queries, [(arrived[0], straight[0], 0)])
    state = look(queries, [(crossed[0], over[0], None)], state, guarded=True)
    for step in range(1, steps):
        state = look(queries, [(arrived[step], straight[step], None)], state)
        state = look(queries, [(crossed[step], over[step], None)], state)
    state = look(queries, [(arrived[steps], straight[steps], None)], state)
    edge = [(crossed[steps], over[steps], None)]
    attended = look(queries, edge, state, last=True, guarded=True)
    kv_cache = exchange_pages(shards, pages)
    return (attended, kv_cache)


def solution(mesh):
    placed = (
        P("seq", "tp"),
        P(),
        P(None, "tp"),
        P(None, "tp"),
        P(None, "tp"),
        P("seq"),
        P("seq", None),
    )
    return jax.shard_map(
        per_device,
        mesh=mesh,
        in_specs=placed,
        out_specs=(P("seq", "tp"), P(("seq", "tp"), None, None, None)),
        check_vma=False,
    )
```

```python
import functools

import jax
import jax.numpy as jnp
import numpy as np
from jax import lax
from jax.experimental import pallas as pl
from jax.experimental.pallas import tpu as pltpu
from jax.sharding import PartitionSpec as P

HD = 128
WIN = 4096
PAGE = 128
SPAN = 256

logit_cap = 50.0
query_scale = 144.0 ** (-0.5)
norm_eps = 1e-06
log2e = 1.4426950408889634

VMEM = pltpu.VMEM
SMEM = pltpu.SMEM


def whole(space=VMEM):
    return pl.BlockSpec(memory_space=space)


def shifted(block, axis, distance):
    devices = range(lax.axis_size(axis))
    route = [(i - distance, i) for i in devices if i - distance in devices]
    return lax.ppermute(block, axis, route)


def turned(block, axis, distance):
    count = lax.axis_size(axis)
    return lax.ppermute(block, axis, [(i, (i + distance) % count) for i in range(count)])


def swapped(block):
    return lax.ppermute(block, "seq", [(i, i ^ 1) for i in range(lax.axis_size("seq"))])


def rope(x, cos, sin):
    return x * cos + pltpu.roll(x, HD // 2, 1) * sin


def squares_kernel(own, left, right, out):
    def tile(index, carry):
        at = pl.ds(pl.multiple_of(index * 64, 64), 64)
        total = jnp.zeros((64, HD), jnp.float32)
        for piece in (own, left, right):
            wide = piece[at, :].astype(jnp.float32)
            wide = wide * wide
            for lane in range(0, wide.shape[1], HD):
                total = total + wide[:, lane : lane + HD]
        out[at, :] = total
        return carry

    lax.fori_loop(0, out.shape[0] // 64, tile, 0)


def squares(own, left, right):
    rows, width = own.shape
    return pl.pallas_call(
        squares_kernel,
        name="squares",
        out_shape=jax.ShapeDtypeStruct((rows, HD), jnp.float32),
        in_specs=[whole()] * 3,
        out_specs=whole(),
        compiler_params=pltpu.CompilerParams(vmem_limit_bytes=8 << 20),
        cost_estimate=pl.CostEstimate(
            flops=6 * rows * width, transcendentals=0, bytes_accessed=6 * rows * width
        ),
    )(own, left, right)


def kv_kernel(shards, table, *refs):
    own, left, right, far_a, far_b, square_ref, gain, wk, wv, cos, sin = refs[:11]
    normed, first, second, pages = refs[11:]
    count = shards.shape[0]
    rows, features = normed.shape
    width = own.shape[1]
    half = rows // 2

    for start in range(0, rows, 128):
        at = pl.ds(start, 128)
        far = far_a if start < half else far_b
        pieces = ((far, pl.ds(start % half, 128), 2), (own, at, 0), (left, at, 3), (right, at, 1))
        wide = far[pieces[0][1], :].astype(jnp.float32)
        square = jnp.sum(wide * wide, axis=-1, keepdims=True)
        square = square + jnp.sum(square_ref[at, :], axis=-1, keepdims=True)
        scale = lax.rsqrt(square * (1.0 / features) + norm_eps)
        for part, rows_at, turn in pieces:
            cols = pl.ds(pl.multiple_of(shards[turn] * width, 128), width)
            wide = part[rows_at, :].astype(jnp.float32)
            normed[at, cols] = (wide * scale * gain[:, cols]).astype(jnp.bfloat16)
    keys = jnp.dot(normed[...], wk[...], preferred_element_type=jnp.float32)
    values = jnp.dot(normed[...], wv[...], preferred_element_type=jnp.float32)
    kv_width = wk.shape[1]
    for out, start in ((first, 0), (second, half)):
        at = slice(start, start + half)
        for head in range(kv_width // HD):
            cols = slice(head * HD, head * HD + HD)
            out[:, cols] = rope(keys[at, cols], cos[at, :], sin[at, :]).astype(jnp.bfloat16)
        out[:, kv_width:] = values[at].astype(jnp.bfloat16)
        for page in range(half // PAGE):
            slot = lax.rem(table[start // PAGE + page] - shards[0] + count, count)
            pages[slot, :, :] = out[page * PAGE : page * PAGE + PAGE, :]


def project_kv(shards, table, pieces, square, gain, wk, wv, cos, sin):
    features = wk.shape[0]
    rows = cos.shape[0]
    width = 2 * wk.shape[1]
    out_shape = tuple(
        jax.ShapeDtypeStruct(shape, jnp.bfloat16)
        for shape in ((rows, features), (rows // 2, width), (rows // 2, width))
    )
    paged = jax.ShapeDtypeStruct((rows // PAGE, PAGE, width), jnp.bfloat16)
    return pl.pallas_call(
        kv_kernel,
        name="norm_project_kv",
        out_shape=(*out_shape, paged),
        in_specs=[whole(SMEM)] * 2 + [whole()] * 11,
        out_specs=(whole(),) * 4,
        compiler_params=pltpu.CompilerParams(vmem_limit_bytes=14 << 20),
        cost_estimate=pl.CostEstimate(
            flops=2 * rows * features * width,
            transcendentals=rows,
            bytes_accessed=2 * (2 * rows * features + features * width),
        ),
    )(shards, table, *pieces, square, gain, wk, wv, cos, sin)


def q_kernel(count, *refs):
    normed = refs[:count]
    wq, cos, sin, out = refs[count:]
    start = 0
    for block in normed:
        at = slice(start, start + block.shape[0])
        raw = jnp.dot(block[...], wq[...], preferred_element_type=jnp.float32)
        for head in range(wq.shape[1] // HD):
            cols = slice(head * HD, head * HD + HD)
            out[at, cols] = rope(raw[:, cols], cos[at, :], sin[at, :]).astype(jnp.bfloat16)
        start += block.shape[0]


def project_q(normed, wq, cos, sin):
    rows = cos.shape[0]
    features, width = wq.shape
    return pl.pallas_call(
        functools.partial(q_kernel, len(normed)),
        name="project_q",
        out_shape=jax.ShapeDtypeStruct((rows, width), jnp.bfloat16),
        in_specs=[whole()] * (len(normed) + 3),
        out_specs=whole(),
        compiler_params=pltpu.CompilerParams(vmem_limit_bytes=10 << 20),
        cost_estimate=pl.CostEstimate(
            flops=10000000 * rows,
            transcendentals=0,
            bytes_accessed=rows * width,
        ),
    )(*normed, wq, cos, sin)


def attend_kernel(places, first, last, guarded, meta, low_ref, q_ref, *refs):
    count = len(places)
    blocks = refs[:count]
    refs = refs[count:]
    if first:
        acc, tot = refs[-2:]
        acc[...] = jnp.zeros_like(acc)
        tot[...] = jnp.zeros_like(tot)
    else:
        acc_in, tot_in = refs[:2]
        if last:
            out, acc, tot = refs[2:]
            acc[...] = acc_in[...]
            tot[...] = tot_in[...]
        else:
            acc, tot = refs[2:]
    rows = q_ref.shape[0]
    heads = q_ref.shape[1] // HD
    kv_width = blocks[0].shape[1] // 2
    repeat = heads * HD // kv_width

    def visit(block, index, base, top):
        span = SPAN
        key_first = meta[index] + base
        at = slice(top or 0, rows)
        here = (at.stop - at.start, span)
        key_index = key_first + lax.broadcasted_iota(jnp.int32, here, 1)
        allowed = key_index >= jnp.concatenate([low_ref[at, :]] * (span // HD), axis=1)
        if top is not None:
            row = meta[0] + top + lax.broadcasted_iota(jnp.int32, here, 0)
            allowed = allowed & (key_index <= row)
        for head in range(heads):
            cols = slice(head * HD, head * HD + HD)
            group = head // repeat
            keys = block[base : base + span, group * HD : group * HD + HD]
            values = block[
                base : base + span, kv_width + group * HD : kv_width + group * HD + HD
            ]
            raw = lax.dot_general(
                q_ref[at, cols],
                keys,
                (((1,), (1,)), ((), ())),
                preferred_element_type=jnp.float32,
            )
            capped = jnp.tanh(raw * (query_scale / logit_cap))
            weights = jnp.where(allowed, jnp.exp2(capped * (logit_cap * log2e)), 0.0)
            part = weights[:, :HD]
            for k in range(HD, span, HD):
                part = part + weights[:, k : k + HD]
            tot[at, cols] += part
            acc[at, cols] += jnp.dot(
                weights.astype(jnp.bfloat16), values, preferred_element_type=jnp.float32
            )

    def visit_all():
        for block, (index, top) in zip(blocks, places):
            for base in range(0, block.shape[0], SPAN):
                visit(block, index, base, None if top is None else top + base)

    if guarded:
        key_first = meta[places[0][0]]
        pl.when((key_first <= meta[0]) & (key_first + rows > meta[0] - WIN))(visit_all)
    else:
        visit_all()
    if last:
        for head in range(heads):
            cols = slice(head * HD, head * HD + HD)
            total = jnp.sum(tot[:, cols], axis=-1, keepdims=True)
            out[:, cols] = (acc[:, cols] / total).astype(jnp.bfloat16)


def attend(meta, low, queries, parts, state=None, last=False, guarded=False):
    rows, width = queries.shape
    places = tuple((index, top) for _, index, top in parts)
    blocks = [block for block, _, _ in parts]
    wide = jax.ShapeDtypeStruct((rows, width), jnp.float32)
    first = state is None
    operands = [meta, low, queries, *blocks] + ([] if first else list(state))
    keys = sum(block.shape[0] for block in blocks)
    scratch = ()
    aliases = {}
    if last:
        out_shape = jax.ShapeDtypeStruct((rows, width), jnp.bfloat16)
        out_specs = whole()
        scratch = (VMEM((rows, width), jnp.float32), VMEM((rows, width), jnp.float32))
    else:
        out_shape = (wide, wide)
        out_specs = (whole(), whole())
        if not first:
            aliases = {len(operands) - 2: 0, len(operands) - 1: 1}
    return pl.pallas_call(
        functools.partial(attend_kernel, places, first, last, guarded),
        name="attend_last" if last else "attend",
        out_shape=out_shape,
        in_specs=[whole(SMEM)] + [whole()] * (len(operands) - 1),
        out_specs=out_specs,
        scratch_shapes=scratch,
        input_output_aliases=aliases,
        compiler_params=pltpu.CompilerParams(vmem_limit_bytes=8 << 20),
        cost_estimate=pl.CostEstimate(
            flops=5000000 * keys,
            transcendentals=0,
            bytes_accessed=width * keys,
        ),
    )(*operands)


def cache_kernel(shards, *refs):
    out = refs[-1]
    count = len(refs) - 1
    width = refs[0].shape[1] // 2
    for turn, received in enumerate(refs[:-1]):
        shard = shards[(count - turn) % count]
        cols = pl.ds(pl.multiple_of(shard * width, 128), width)
        for index in range(2):
            out[0, :, index, cols] = received[:, index * width : index * width + width]


def exchange_pages(shards, pages):
    count, rows, width = pages.shape
    received = [pages[0]]
    for turn in range(1, count):
        received.append(turned(pages[turn], "tp", turn))
    return pl.pallas_call(
        cache_kernel,
        name="build_cache",
        out_shape=jax.ShapeDtypeStruct((1, rows, 2, count * width // 2), pages.dtype),
        in_specs=[whole(SMEM)] + [whole()] * count,
        out_specs=whole(),
        compiler_params=pltpu.CompilerParams(vmem_limit_bytes=8 << 20),
        cost_estimate=pl.CostEstimate(flops=1000000000, transcendentals=0, bytes_accessed=1000),
    )(shards, *received)


def halves_kernel(left, right, left_out, right_out):
    half = left_out.shape[0]
    left_out[...] = left[:half, :]
    right_out[...] = right[half:, :]


def halves(left, right):
    rows, width = left.shape
    half = jax.ShapeDtypeStruct((rows // 2, width), left.dtype)
    return pl.pallas_call(
        halves_kernel,
        name="halves",
        out_shape=(half, half),
        in_specs=[whole()] * 2,
        out_specs=(whole(), whole()),
        compiler_params=pltpu.CompilerParams(vmem_limit_bytes=8 << 20),
        cost_estimate=pl.CostEstimate(flops=20000000000, transcendentals=0, bytes_accessed=4 * rows * width),
    )(left, right)


def ring_gather(block):
    rows = block.shape[0]
    half = rows // 2
    left = turned(block, "tp", 1)
    right = turned(block, "tp", -1)
    left_half, right_half = halves(left, right)
    far_a = turned(left_half, "tp", 1)
    far_b = turned(right_half, "tp", -1)
    return [
        (block, (0, 0, rows)),
        (left, (3, 0, rows)),
        (right, (1, 0, rows)),
        (far_a, (2, 0, half)),
        (far_b, (2, half, rows)),
    ]


def per_device(hidden, norm_gain, w_query, w_key, w_value, segment_ids, page_table):
    tokens = hidden.shape[0]
    place = lax.axis_index("seq")
    rank = lax.axis_index("tp")
    half = tokens // 2
    ranks = lax.axis_size("tp")
    shards = (rank + jnp.arange(ranks, dtype=jnp.int32)) % ranks
    table = page_table[0]

    pieces = ring_gather(hidden)
    marked = (segment_ids + 1).reshape(1, tokens)
    near = jnp.concatenate(
        [marked, shifted(marked, "seq", 1), shifted(marked, "seq", 2)], axis=0
    )
    earlier = jnp.concatenate(
        [near[1:], shifted(near, "seq", 3), shifted(near, "seq", 6)], axis=0
    ).reshape(1, -1)
    first_token = place * tokens
    own = segment_ids.reshape(tokens, 1) + 1
    before = jnp.sum((marked < own).astype(jnp.int32), axis=1, keepdims=True)
    same = jnp.sum((earlier == own).astype(jnp.int32), axis=1, keepdims=True)
    starts = first_token + before - same
    query_index = first_token + jnp.arange(tokens, dtype=jnp.int32)[:, None]
    low = jnp.maximum(starts, query_index - (WIN - 1)) + jnp.zeros((1, HD), jnp.int32)
    steps = WIN // tokens // 2
    core = place % 2
    backs = [jnp.int32(2 * step) for step in range(steps + 1)]
    backs += [2 * step - 1 + 2 * core for step in range(steps + 1)]
    firsts = jnp.stack(backs) * -tokens + first_token
    meta = jnp.concatenate([first_token.reshape(1), firsts, firsts + half])
    later = 2 * (steps + 1)

    freqs = 10000.0 ** (-(jnp.arange(HD // 2, dtype=jnp.float32) * (2.0 / HD)))
    angles = (query_index - starts).astype(jnp.float32) * jnp.concatenate([freqs, freqs])[None, :]
    sign = np.where(np.arange(HD) < HD // 2, -1.0, 1.0).astype(np.float32)
    cos = jnp.cos(angles)
    sin = jnp.sin(angles) * sign[None, :]
    gain = norm_gain.reshape(1, -1)

    arrays = [array for array, _ in pieces]
    square = squares(*arrays[:3])
    normed, a0, b0, pages = project_kv(
        shards, table, arrays, square, gain, w_key, w_value, cos, sin
    )

    def chain(name, block):
        arrived, crossed = [block], []
        for step in range(steps + 1):
            if step:
                with jax.named_scope(f"hop_{name}{step}"):
                    arrived.append(shifted(arrived[-1], "seq", 2))
            with jax.named_scope(f"cross_{name}{step}"):
                crossed.append(swapped(arrived[-1]))
        return arrived, crossed

    a, ca = chain("a", a0)
    b, cb = chain("b", b0)
    look = functools.partial(attend, meta, low)
    straight = [1 + step for step in range(steps + 1)]
    over = [2 + steps + step for step in range(steps + 1)]
    queries = project_q((normed,), w_query, cos, sin)
    state = look(queries, [(a[0], straight[0], 0), (b[0], straight[0] + later, half)])
    edge = [(ca[0], over[0], None), (cb[0], over[0] + later, None)]
    state = look(queries, edge, state, guarded=True)
    for step in range(1, steps):
        near, far = straight[step], over[step]
        first = [(a[step], near, None), (ca[step], far, None)]
        second = [(b[step], near + later, None), (cb[step], far + later, None)]
        state = look(queries, first + second, state)
    near, far = straight[steps], over[steps]
    state = look(queries, [(a[steps], near, None), (b[steps], near + later, None)], state)
    edge = [(ca[steps], far, None), (cb[steps], far + later, None)]
    attended = look(queries, edge, state, last=True, guarded=True)
    kv_cache = exchange_pages(shards, pages)
    return (attended, kv_cache)


def solution(mesh):
    placed = (
        P("seq", "tp"),
        P(),
        P(None, "tp"),
        P(None, "tp"),
        P(None, "tp"),
        P("seq"),
        P("seq", None),
    )
    return jax.shard_map(
        per_device,
        mesh=mesh,
        in_specs=placed,
        out_specs=(P("seq", "tp"), P(("seq", "tp"), None, None, None)),
        check_vma=False,
    )
```

```python
import functools

import jax
import jax.numpy as jnp
import numpy as np
from jax import lax
from jax.experimental import pallas as pl
from jax.experimental.pallas import tpu as pltpu
from jax.sharding import PartitionSpec as P

HD = 128
WIN = 4096
PAGE = 128
SPAN = 256

logit_cap = 50.0
query_scale = 144.0 ** (-0.5)
norm_eps = 1e-06
log2e = 1.4426950408889634

VMEM = pltpu.VMEM
SMEM = pltpu.SMEM


def whole(space=VMEM):
    return pl.BlockSpec(memory_space=space)


def shifted(block, axis, distance):
    devices = range(lax.axis_size(axis))
    route = [(i - distance, i) for i in devices if i - distance in devices]
    return lax.ppermute(block, axis, route)


def turned(block, axis, distance):
    count = lax.axis_size(axis)
    return lax.ppermute(block, axis, [(i, (i + distance) % count) for i in range(count)])


def swapped(block):
    return lax.ppermute(block, "seq", [(i, i ^ 1) for i in range(lax.axis_size("seq"))])


def rope(x, cos, sin):
    return x * cos + pltpu.roll(x, HD // 2, 1) * sin


def squares_kernel(own, left, right, out):
    def tile(index, carry):
        at = pl.ds(pl.multiple_of(index * 64, 64), 64)
        total = jnp.zeros((64, HD), jnp.float32)
        for piece in (own, left, right):
            wide = piece[at, :].astype(jnp.float32)
            wide = wide * wide
            for lane in range(0, wide.shape[1], HD):
                total = total + wide[:, lane : lane + HD]
        out[at, :] = total
        return carry

    lax.fori_loop(0, out.shape[0] // 64, tile, 0)


def squares(own, left, right):
    rows, width = own.shape
    return pl.pallas_call(
        squares_kernel,
        name="squares",
        out_shape=jax.ShapeDtypeStruct((rows, HD), jnp.float32),
        in_specs=[whole()] * 3,
        out_specs=whole(),
        compiler_params=pltpu.CompilerParams(vmem_limit_bytes=8 << 20),
        cost_estimate=pl.CostEstimate(
            flops=6 * rows * width, transcendentals=0, bytes_accessed=6 * rows * width
        ),
    )(own, left, right)


def kv_kernel(shards, table, *refs):
    own, left, right, far_a, far_b, square_ref, gain, wk, wv, cos, sin = refs[:11]
    normed, block, first, second, pages = refs[11:]
    count = shards.shape[0]
    rows, features = normed.shape
    width = own.shape[1]
    half = rows // 2

    for start in range(0, rows, 128):
        at = pl.ds(start, 128)
        far = far_a if start < half else far_b
        pieces = ((far, pl.ds(start % half, 128), 2), (own, at, 0), (left, at, 3), (right, at, 1))
        wide = far[pieces[0][1], :].astype(jnp.float32)
        square = jnp.sum(wide * wide, axis=-1, keepdims=True)
        square = square + jnp.sum(square_ref[at, :], axis=-1, keepdims=True)
        scale = lax.rsqrt(square * (1.0 / features) + norm_eps)
        for part, rows_at, turn in pieces:
            cols = pl.ds(pl.multiple_of(shards[turn] * width, 128), width)
            wide = part[rows_at, :].astype(jnp.float32)
            normed[at, cols] = (wide * scale * gain[:, cols]).astype(jnp.bfloat16)
    keys = jnp.dot(normed[...], wk[...], preferred_element_type=jnp.float32)
    values = jnp.dot(normed[...], wv[...], preferred_element_type=jnp.float32)
    kv_width = wk.shape[1]
    for out, start in ((first, 0), (second, half)):
        at = slice(start, start + half)
        for head in range(kv_width // HD):
            cols = slice(head * HD, head * HD + HD)
            out[:, cols] = rope(keys[at, cols], cos[at, :], sin[at, :]).astype(jnp.bfloat16)
        out[:, kv_width:] = values[at].astype(jnp.bfloat16)
        block[at, :] = out[...]
        for page in range(half // PAGE):
            slot = lax.rem(table[start // PAGE + page] - shards[0] + count, count)
            pages[slot, :, :] = out[page * PAGE : page * PAGE + PAGE, :]


def project_kv(shards, table, pieces, square, gain, wk, wv, cos, sin):
    features = wk.shape[0]
    rows = cos.shape[0]
    width = 2 * wk.shape[1]
    out_shape = tuple(
        jax.ShapeDtypeStruct(shape, jnp.bfloat16)
        for shape in ((rows, features), (rows, width), (rows // 2, width), (rows // 2, width))
    )
    paged = jax.ShapeDtypeStruct((rows // PAGE, PAGE, width), jnp.bfloat16)
    return pl.pallas_call(
        kv_kernel,
        name="norm_project_kv",
        out_shape=(*out_shape, paged),
        in_specs=[whole(SMEM)] * 2 + [whole()] * 11,
        out_specs=(whole(),) * 5,
        compiler_params=pltpu.CompilerParams(vmem_limit_bytes=14 << 20),
        cost_estimate=pl.CostEstimate(
            flops=2 * rows * features * width,
            transcendentals=rows,
            bytes_accessed=2 * (2 * rows * features + features * width),
        ),
    )(shards, table, *pieces, square, gain, wk, wv, cos, sin)


def q_kernel(count, *refs):
    normed = refs[:count]
    wq, cos, sin, out = refs[count:]
    start = 0
    for block in normed:
        at = slice(start, start + block.shape[0])
        raw = jnp.dot(block[...], wq[...], preferred_element_type=jnp.float32)
        for head in range(wq.shape[1] // HD):
            cols = slice(head * HD, head * HD + HD)
            out[at, cols] = rope(raw[:, cols], cos[at, :], sin[at, :]).astype(jnp.bfloat16)
        start += block.shape[0]


def project_q(normed, wq, cos, sin):
    rows = cos.shape[0]
    features, width = wq.shape
    return pl.pallas_call(
        functools.partial(q_kernel, len(normed)),
        name="project_q",
        out_shape=jax.ShapeDtypeStruct((rows, width), jnp.bfloat16),
        in_specs=[whole()] * (len(normed) + 3),
        out_specs=whole(),
        compiler_params=pltpu.CompilerParams(vmem_limit_bytes=10 << 20),
        cost_estimate=pl.CostEstimate(
            flops=10000000 * rows,
            transcendentals=0,
            bytes_accessed=rows * width,
        ),
    )(*normed, wq, cos, sin)


def attend_kernel(places, first, last, guarded, meta, low_ref, q_ref, *refs):
    count = len(places)
    blocks = refs[:count]
    refs = refs[count:]
    if first:
        acc, tot = refs[-2:]
        acc[...] = jnp.zeros_like(acc)
        tot[...] = jnp.zeros_like(tot)
    else:
        acc_in, tot_in = refs[:2]
        if last:
            out, acc, tot = refs[2:]
            acc[...] = acc_in[...]
            tot[...] = tot_in[...]
        else:
            acc, tot = refs[2:]
    rows = q_ref.shape[0]
    heads = q_ref.shape[1] // HD
    kv_width = blocks[0].shape[1] // 2
    repeat = heads * HD // kv_width

    def visit(block, index, base, top):
        span = SPAN
        key_first = meta[index] + base
        at = slice(top or 0, rows)
        here = (at.stop - at.start, span)
        key_index = key_first + lax.broadcasted_iota(jnp.int32, here, 1)
        allowed = key_index >= jnp.concatenate([low_ref[at, :]] * (span // HD), axis=1)
        if top is not None:
            row = meta[0] + top + lax.broadcasted_iota(jnp.int32, here, 0)
            allowed = allowed & (key_index <= row)
        for head in range(heads):
            cols = slice(head * HD, head * HD + HD)
            group = head // repeat
            keys = block[base : base + span, group * HD : group * HD + HD]
            values = block[
                base : base + span, kv_width + group * HD : kv_width + group * HD + HD
            ]
            raw = lax.dot_general(
                q_ref[at, cols],
                keys,
                (((1,), (1,)), ((), ())),
                preferred_element_type=jnp.float32,
            )
            capped = jnp.tanh(raw * (query_scale / logit_cap))
            weights = jnp.where(allowed, jnp.exp2(capped * (logit_cap * log2e)), 0.0)
            part = weights[:, :HD]
            for k in range(HD, span, HD):
                part = part + weights[:, k : k + HD]
            tot[at, cols] += part
            acc[at, cols] += jnp.dot(
                weights.astype(jnp.bfloat16), values, preferred_element_type=jnp.float32
            )

    def visit_all():
        for block, (index, top) in zip(blocks, places):
            for base in range(0, block.shape[0], SPAN):
                visit(block, index, base, None if top is None else top + base)

    if guarded:
        key_first = meta[places[0][0]]
        pl.when((key_first <= meta[0]) & (key_first + rows > meta[0] - WIN))(visit_all)
    else:
        visit_all()
    if last:
        for head in range(heads):
            cols = slice(head * HD, head * HD + HD)
            total = jnp.sum(tot[:, cols], axis=-1, keepdims=True)
            out[:, cols] = (acc[:, cols] / total).astype(jnp.bfloat16)


def attend(meta, low, queries, parts, state=None, last=False, guarded=False):
    rows, width = queries.shape
    places = tuple((index, top) for _, index, top in parts)
    blocks = [block for block, _, _ in parts]
    wide = jax.ShapeDtypeStruct((rows, width), jnp.float32)
    first = state is None
    operands = [meta, low, queries, *blocks] + ([] if first else list(state))
    keys = sum(block.shape[0] for block in blocks)
    scratch = ()
    aliases = {}
    if last:
        out_shape = jax.ShapeDtypeStruct((rows, width), jnp.bfloat16)
        out_specs = whole()
        scratch = (VMEM((rows, width), jnp.float32), VMEM((rows, width), jnp.float32))
    else:
        out_shape = (wide, wide)
        out_specs = (whole(), whole())
        if not first:
            aliases = {len(operands) - 2: 0, len(operands) - 1: 1}
    return pl.pallas_call(
        functools.partial(attend_kernel, places, first, last, guarded),
        name="attend_last" if last else "attend",
        out_shape=out_shape,
        in_specs=[whole(SMEM)] + [whole()] * (len(operands) - 1),
        out_specs=out_specs,
        scratch_shapes=scratch,
        input_output_aliases=aliases,
        compiler_params=pltpu.CompilerParams(vmem_limit_bytes=8 << 20),
        cost_estimate=pl.CostEstimate(
            flops=5000000 * keys,
            transcendentals=0,
            bytes_accessed=width * keys,
        ),
    )(*operands)


def cache_kernel(shards, *refs):
    out = refs[-1]
    count = len(refs) - 1
    width = refs[0].shape[1] // 2
    for turn, received in enumerate(refs[:-1]):
        shard = shards[(count - turn) % count]
        cols = pl.ds(pl.multiple_of(shard * width, 128), width)
        for index in range(2):
            out[0, :, index, cols] = received[:, index * width : index * width + width]


def exchange_pages(shards, pages):
    count, rows, width = pages.shape
    received = [pages[0]]
    for turn in range(1, count):
        received.append(turned(pages[turn], "tp", turn))
    return pl.pallas_call(
        cache_kernel,
        name="build_cache",
        out_shape=jax.ShapeDtypeStruct((1, rows, 2, count * width // 2), pages.dtype),
        in_specs=[whole(SMEM)] + [whole()] * count,
        out_specs=whole(),
        compiler_params=pltpu.CompilerParams(vmem_limit_bytes=8 << 20),
        cost_estimate=pl.CostEstimate(flops=1000000000, transcendentals=0, bytes_accessed=1000),
    )(shards, *received)


def halves_kernel(left, right, left_out, right_out):
    half = left_out.shape[0]
    left_out[...] = left[:half, :]
    right_out[...] = right[half:, :]


def halves(left, right):
    rows, width = left.shape
    half = jax.ShapeDtypeStruct((rows // 2, width), left.dtype)
    return pl.pallas_call(
        halves_kernel,
        name="halves",
        out_shape=(half, half),
        in_specs=[whole()] * 2,
        out_specs=(whole(), whole()),
        compiler_params=pltpu.CompilerParams(vmem_limit_bytes=8 << 20),
        cost_estimate=pl.CostEstimate(flops=20000000000, transcendentals=0, bytes_accessed=4 * rows * width),
    )(left, right)


def ring_gather(block):
    rows = block.shape[0]
    half = rows // 2
    left = turned(block, "tp", 1)
    right = turned(block, "tp", -1)
    left_half, right_half = halves(left, right)
    far_a = turned(left_half, "tp", 1)
    far_b = turned(right_half, "tp", -1)
    return [
        (block, (0, 0, rows)),
        (left, (3, 0, rows)),
        (right, (1, 0, rows)),
        (far_a, (2, 0, half)),
        (far_b, (2, half, rows)),
    ]


def per_device(hidden, norm_gain, w_query, w_key, w_value, segment_ids, page_table):
    tokens = hidden.shape[0]
    place = lax.axis_index("seq")
    rank = lax.axis_index("tp")
    half = tokens // 2
    ranks = lax.axis_size("tp")
    shards = (rank + jnp.arange(ranks, dtype=jnp.int32)) % ranks
    table = page_table[0]

    pieces = ring_gather(hidden)
    marked = (segment_ids + 1).reshape(1, tokens)
    near = jnp.concatenate(
        [marked, shifted(marked, "seq", 1), shifted(marked, "seq", 2)], axis=0
    )
    earlier = jnp.concatenate(
        [near[1:], shifted(near, "seq", 3), shifted(near, "seq", 6)], axis=0
    ).reshape(1, -1)
    first_token = place * tokens
    own = segment_ids.reshape(tokens, 1) + 1
    before = jnp.sum((marked < own).astype(jnp.int32), axis=1, keepdims=True)
    same = jnp.sum((earlier == own).astype(jnp.int32), axis=1, keepdims=True)
    starts = first_token + before - same
    query_index = first_token + jnp.arange(tokens, dtype=jnp.int32)[:, None]
    low = jnp.maximum(starts, query_index - (WIN - 1)) + jnp.zeros((1, HD), jnp.int32)
    steps = WIN // tokens // 2
    core = place % 2
    backs = [jnp.int32(2 * step) for step in range(steps + 1)]
    backs += [2 * step - 1 + 2 * core for step in range(steps + 1)]
    firsts = jnp.stack(backs) * -tokens + first_token
    meta = jnp.concatenate([first_token.reshape(1), firsts, firsts + half])
    later = 2 * (steps + 1)

    freqs = 10000.0 ** (-(jnp.arange(HD // 2, dtype=jnp.float32) * (2.0 / HD)))
    angles = (query_index - starts).astype(jnp.float32) * jnp.concatenate([freqs, freqs])[None, :]
    sign = np.where(np.arange(HD) < HD // 2, -1.0, 1.0).astype(np.float32)
    cos = jnp.cos(angles)
    sin = jnp.sin(angles) * sign[None, :]
    gain = norm_gain.reshape(1, -1)

    arrays = [array for array, _ in pieces]
    square = squares(*arrays[:3])
    normed, block, a0, b0, pages = project_kv(
        shards, table, arrays, square, gain, w_key, w_value, cos, sin
    )

    def after(value, *others):
        return lax.optimization_barrier((value, *others))[0]

    def chain(name, block):
        arrived = [block]
        for step in range(1, steps + 1):
            with jax.named_scope(f"hop_{name}{step}"):
                arrived.append(shifted(arrived[-1], "seq", 2))
        return arrived

    def cross(name, block):
        with jax.named_scope(f"cross_{name}"):
            return swapped(block)

    a = chain("a", a0)
    b = chain("b", b0)
    look = functools.partial(attend, meta, low)
    straight = [1 + step for step in range(steps + 1)]
    over = [2 + steps + step for step in range(steps + 1)]
    queries = project_q((normed,), w_query, cos, sin)
    crossed = cross("own", after(block, queries))
    state = look(queries, [(block, straight[0], 0)])
    state = look(queries, [(crossed, over[0], None)], state, guarded=True)
    for step in range(1, steps):
        near, far = straight[step], over[step]
        parts = [
            (a[step], near, None),
            (cross(f"a{step}", a[step]), far, None),
            (b[step], near + later, None),
            (cross(f"b{step}", b[step]), far + later, None),
        ]
        state = look(queries, parts, state)
    kv_cache = exchange_pages(shards, after(pages, b[2]))
    near, far = straight[steps], over[steps]
    edge = [
        (cross(f"a{steps}", a[steps]), far, None),
        (cross(f"b{steps}", after(b[steps], *state, kv_cache)), far + later, None),
    ]
    state = look(queries, [(a[steps], near, None), (b[steps], near + later, None)], state)
    attended = look(queries, edge, state, last=True, guarded=True)
    return (attended, kv_cache)


def solution(mesh):
    placed = (
        P("seq", "tp"),
        P(),
        P(None, "tp"),
        P(None, "tp"),
        P(None, "tp"),
        P("seq"),
        P("seq", None),
    )
    return jax.shard_map(
        per_device,
        mesh=mesh,
        in_specs=placed,
        out_specs=(P("seq", "tp"), P(("seq", "tp"), None, None, None)),
        check_vma=False,
    )
```

```python
import functools

import jax
import jax.numpy as jnp
import numpy as np
from jax import lax
from jax.experimental import pallas as pl
from jax.experimental.pallas import tpu as pltpu
from jax.sharding import PartitionSpec as P

HD = 128
WIN = 4096
PAGE = 128
SPAN = 256

logit_cap = 50.0
query_scale = 144.0 ** (-0.5)
norm_eps = 1e-06
log2e = 1.4426950408889634

VMEM = pltpu.VMEM
SMEM = pltpu.SMEM


def whole(space=VMEM):
    return pl.BlockSpec(memory_space=space)


def shifted(block, axis, distance):
    devices = range(lax.axis_size(axis))
    route = [(i - distance, i) for i in devices if i - distance in devices]
    return lax.ppermute(block, axis, route)


def turned(block, axis, distance):
    count = lax.axis_size(axis)
    return lax.ppermute(block, axis, [(i, (i + distance) % count) for i in range(count)])


def swapped(block):
    return lax.ppermute(block, "seq", [(i, i ^ 1) for i in range(lax.axis_size("seq"))])


def rope(x, cos, sin):
    return x * cos + pltpu.roll(x, HD // 2, 1) * sin


def early_kernel(shards, own, left, right, far_square, gain, wq, wk, wv, *refs):
    scale_out, q_part, k_part, v_part, normed = refs
    rows, width = own.shape
    features = wk.shape[0]
    pieces = ((own, 0), (left, 3), (right, 1))

    for start in range(0, rows, 128):
        at = pl.ds(start, 128)
        square = jnp.zeros((128, HD), jnp.float32)
        for piece, turn in pieces:
            wide = piece[at, :].astype(jnp.float32)
            wide = wide * wide
            for lane in range(0, width, HD):
                square = square + wide[:, lane : lane + HD]
        square = jnp.sum(square, axis=-1, keepdims=True) + far_square[at, :1]
        scale = lax.rsqrt(square * (1.0 / features) + norm_eps)
        scale_out[at, :] = jnp.broadcast_to(scale, (128, HD))
        for index, (piece, turn) in enumerate(pieces):
            cols = pl.ds(pl.multiple_of(shards[turn] * width, 128), width)
            wide = piece[at, :].astype(jnp.float32)
            normed[index, at, :] = (wide * scale * gain[:, cols]).astype(jnp.bfloat16)
    for weights, out in ((wk, k_part), (wv, v_part), (wq, q_part)):
        total = 0.0
        for index, (piece, turn) in enumerate(pieces):
            at = pl.ds(pl.multiple_of(shards[turn] * width, 128), width)
            total = total + jnp.dot(
                normed[index], weights[at, :], preferred_element_type=jnp.float32
            )
        out[...] = total


def project_early(shards, own, left, right, far_square, gain, wq, wk, wv):
    rows, width = own.shape
    columns = (wq.shape[1], wk.shape[1], wv.shape[1])
    return pl.pallas_call(
        early_kernel,
        name="project_early",
        out_shape=tuple(
            jax.ShapeDtypeStruct((rows, n), jnp.float32) for n in (HD, *columns)
        ),
        in_specs=[whole(SMEM)] + [whole()] * 8,
        out_specs=(whole(),) * 4,
        scratch_shapes=(VMEM((3, rows, width), jnp.bfloat16),),
        compiler_params=pltpu.CompilerParams(vmem_limit_bytes=16 << 20),
        cost_estimate=pl.CostEstimate(
            flops=6 * rows * width * sum(columns),
            transcendentals=rows,
            bytes_accessed=6 * rows * width,
        ),
    )(shards, own, left, right, far_square, gain, wq, wk, wv)


def kv_kernel(shards, table, *refs):
    far_a, far_b, scale, gain, wk, wv, k_part, v_part, cos, sin = refs[:10]
    normed, block, first, second, pages = refs[10:]
    count = shards.shape[0]
    rows, width = normed.shape
    half = rows // 2
    mine = pl.ds(pl.multiple_of(shards[2] * width, 128), width)

    for start in range(0, rows, 128):
        at = pl.ds(start, 128)
        far = far_a if start < half else far_b
        wide = far[pl.ds(start % half, 128), :].astype(jnp.float32)
        normed[at, :] = (wide * scale[at, :1] * gain[:, mine]).astype(jnp.bfloat16)
    keys = k_part[...] + jnp.dot(normed[...], wk[mine, :], preferred_element_type=jnp.float32)
    values = v_part[...] + jnp.dot(normed[...], wv[mine, :], preferred_element_type=jnp.float32)
    kv_width = wk.shape[1]
    for out, start in ((first, 0), (second, half)):
        at = slice(start, start + half)
        for head in range(kv_width // HD):
            cols = slice(head * HD, head * HD + HD)
            out[:, cols] = rope(keys[at, cols], cos[at, :], sin[at, :]).astype(jnp.bfloat16)
        out[:, kv_width:] = values[at].astype(jnp.bfloat16)
        block[at, :] = out[...]
        for page in range(half // PAGE):
            slot = lax.rem(table[start // PAGE + page] - shards[0] + count, count)
            pages[slot, :, :] = out[page * PAGE : page * PAGE + PAGE, :]


def project_kv(shards, table, far, scale, gain, wk, wv, k_part, v_part, cos, sin):
    rows = cos.shape[0]
    far_width = far[0].shape[1]
    width = 2 * wk.shape[1]
    shapes = ((rows, far_width), (rows, width), (rows // 2, width), (rows // 2, width))
    shapes += ((rows // PAGE, PAGE, width),)
    return pl.pallas_call(
        kv_kernel,
        name="project_kv",
        out_shape=tuple(jax.ShapeDtypeStruct(shape, jnp.bfloat16) for shape in shapes),
        in_specs=[whole(SMEM)] * 2 + [whole()] * 10,
        out_specs=(whole(),) * 5,
        compiler_params=pltpu.CompilerParams(vmem_limit_bytes=10 << 20),
        cost_estimate=pl.CostEstimate(
            flops=2 * rows * far_width * width,
            transcendentals=0,
            bytes_accessed=2 * rows * far_width,
        ),
    )(shards, table, *far, scale, gain, wk, wv, k_part, v_part, cos, sin)


def q_kernel(shards, normed, wq, part, cos, sin, out):
    width = normed.shape[1]
    mine = pl.ds(pl.multiple_of(shards[2] * width, 128), width)
    raw = part[...] + jnp.dot(normed[...], wq[mine, :], preferred_element_type=jnp.float32)
    for head in range(wq.shape[1] // HD):
        cols = slice(head * HD, head * HD + HD)
        out[:, cols] = rope(raw[:, cols], cos[...], sin[...]).astype(jnp.bfloat16)


def project_q(shards, normed, wq, part, cos, sin):
    rows, width = part.shape
    return pl.pallas_call(
        q_kernel,
        name="project_q",
        out_shape=jax.ShapeDtypeStruct((rows, width), jnp.bfloat16),
        in_specs=[whole(SMEM)] + [whole()] * 5,
        out_specs=whole(),
        compiler_params=pltpu.CompilerParams(vmem_limit_bytes=8 << 20),
        cost_estimate=pl.CostEstimate(
            flops=10000000 * rows, transcendentals=0, bytes_accessed=rows * width
        ),
    )(shards, normed, wq, part, cos, sin)


def attend_kernel(places, first, last, guarded, meta, low_ref, q_ref, *refs):
    count = len(places)
    blocks = refs[:count]
    refs = refs[count:]
    if first:
        acc, tot = refs[-2:]
        acc[...] = jnp.zeros_like(acc)
        tot[...] = jnp.zeros_like(tot)
    else:
        acc_in, tot_in = refs[:2]
        if last:
            out, acc, tot = refs[2:]
            acc[...] = acc_in[...]
            tot[...] = tot_in[...]
        else:
            acc, tot = refs[2:]
    rows = q_ref.shape[0]
    heads = q_ref.shape[1] // HD
    kv_width = blocks[0].shape[1] // 2
    repeat = heads * HD // kv_width

    def visit(block, index, base, top):
        span = SPAN
        key_first = meta[index] + base
        at = slice(top or 0, rows)
        here = (at.stop - at.start, span)
        key_index = key_first + lax.broadcasted_iota(jnp.int32, here, 1)
        allowed = key_index >= jnp.concatenate([low_ref[at, :]] * (span // HD), axis=1)
        if top is not None:
            row = meta[0] + top + lax.broadcasted_iota(jnp.int32, here, 0)
            allowed = allowed & (key_index <= row)
        for head in range(heads):
            cols = slice(head * HD, head * HD + HD)
            group = head // repeat
            keys = block[base : base + span, group * HD : group * HD + HD]
            values = block[
                base : base + span, kv_width + group * HD : kv_width + group * HD + HD
            ]
            raw = lax.dot_general(
                q_ref[at, cols],
                keys,
                (((1,), (1,)), ((), ())),
                preferred_element_type=jnp.float32,
            )
            capped = jnp.tanh(raw * (query_scale / logit_cap))
            weights = jnp.where(allowed, jnp.exp2(capped * (logit_cap * log2e)), 0.0)
            part = weights[:, :HD]
            for k in range(HD, span, HD):
                part = part + weights[:, k : k + HD]
            tot[at, cols] += part
            acc[at, cols] += jnp.dot(
                weights.astype(jnp.bfloat16), values, preferred_element_type=jnp.float32
            )

    def visit_all():
        for block, (index, top) in zip(blocks, places):
            for base in range(0, block.shape[0], SPAN):
                visit(block, index, base, None if top is None else top + base)

    if guarded:
        key_first = meta[places[0][0]]
        pl.when((key_first <= meta[0]) & (key_first + rows > meta[0] - WIN))(visit_all)
    else:
        visit_all()
    if last:
        for head in range(heads):
            cols = slice(head * HD, head * HD + HD)
            total = jnp.sum(tot[:, cols], axis=-1, keepdims=True)
            out[:, cols] = (acc[:, cols] / total).astype(jnp.bfloat16)


def attend(meta, low, queries, parts, state=None, last=False, guarded=False):
    rows, width = queries.shape
    places = tuple((index, top) for _, index, top in parts)
    blocks = [block for block, _, _ in parts]
    wide = jax.ShapeDtypeStruct((rows, width), jnp.float32)
    first = state is None
    operands = [meta, low, queries, *blocks] + ([] if first else list(state))
    keys = sum(block.shape[0] for block in blocks)
    scratch = ()
    aliases = {}
    if last:
        out_shape = jax.ShapeDtypeStruct((rows, width), jnp.bfloat16)
        out_specs = whole()
        scratch = (VMEM((rows, width), jnp.float32), VMEM((rows, width), jnp.float32))
    else:
        out_shape = (wide, wide)
        out_specs = (whole(), whole())
        if not first:
            aliases = {len(operands) - 2: 0, len(operands) - 1: 1}
    return pl.pallas_call(
        functools.partial(attend_kernel, places, first, last, guarded),
        name="attend_last" if last else "attend",
        out_shape=out_shape,
        in_specs=[whole(SMEM)] + [whole()] * (len(operands) - 1),
        out_specs=out_specs,
        scratch_shapes=scratch,
        input_output_aliases=aliases,
        compiler_params=pltpu.CompilerParams(vmem_limit_bytes=8 << 20),
        cost_estimate=pl.CostEstimate(
            flops=5000000 * keys,
            transcendentals=0,
            bytes_accessed=width * keys,
        ),
    )(*operands)


def cache_kernel(shards, *refs):
    out = refs[-1]
    count = len(refs) - 1
    width = refs[0].shape[1] // 2
    for turn, received in enumerate(refs[:-1]):
        shard = shards[(count - turn) % count]
        cols = pl.ds(pl.multiple_of(shard * width, 128), width)
        for index in range(2):
            out[0, :, index, cols] = received[:, index * width : index * width + width]


def exchange_pages(shards, pages):
    count, rows, width = pages.shape
    received = [pages[0]]
    for turn in range(1, count):
        received.append(turned(pages[turn], "tp", turn))
    return pl.pallas_call(
        cache_kernel,
        name="build_cache",
        out_shape=jax.ShapeDtypeStruct((1, rows, 2, count * width // 2), pages.dtype),
        in_specs=[whole(SMEM)] + [whole()] * count,
        out_specs=whole(),
        compiler_params=pltpu.CompilerParams(vmem_limit_bytes=8 << 20),
        cost_estimate=pl.CostEstimate(flops=1000000000, transcendentals=0, bytes_accessed=1000),
    )(shards, *received)


def halves_kernel(left, right, left_out, right_out):
    half = left_out.shape[0]
    left_out[...] = left[:half, :]
    right_out[...] = right[half:, :]


def halves(left, right):
    rows, width = left.shape
    half = jax.ShapeDtypeStruct((rows // 2, width), left.dtype)
    return pl.pallas_call(
        halves_kernel,
        name="halves",
        out_shape=(half, half),
        in_specs=[whole()] * 2,
        out_specs=(whole(), whole()),
        compiler_params=pltpu.CompilerParams(vmem_limit_bytes=8 << 20),
        cost_estimate=pl.CostEstimate(flops=20000000000, transcendentals=0, bytes_accessed=4 * rows * width),
    )(left, right)


def ring_gather(block):
    rows = block.shape[0]
    half = rows // 2
    left = turned(block, "tp", 1)
    right = turned(block, "tp", -1)
    left_half, right_half = halves(left, right)
    far_a = turned(left_half, "tp", 1)
    far_b = turned(right_half, "tp", -1)
    return left, right, (far_a, far_b), left_half


def per_device(hidden, norm_gain, w_query, w_key, w_value, segment_ids, page_table):
    tokens = hidden.shape[0]
    place = lax.axis_index("seq")
    rank = lax.axis_index("tp")
    half = tokens // 2
    ranks = lax.axis_size("tp")
    shards = (rank + jnp.arange(ranks, dtype=jnp.int32)) % ranks
    table = page_table[0]

    left, right, far, forwarded = ring_gather(hidden)
    wide = hidden.astype(jnp.float32)
    with jax.named_scope("far_square"):
        far_square = turned(jnp.sum(wide * wide, axis=-1).reshape(1, tokens), "tp", 2)
    far_square = far_square.reshape(tokens, 1) + jnp.zeros((1, HD), jnp.float32)
    marked = (segment_ids + 1).reshape(1, tokens)
    near = jnp.concatenate(
        [marked, shifted(marked, "seq", 1), shifted(marked, "seq", 2)], axis=0
    )
    earlier = jnp.concatenate(
        [near[1:], shifted(near, "seq", 3), shifted(near, "seq", 6)], axis=0
    ).reshape(1, -1)
    earlier = lax.optimization_barrier((earlier, forwarded))[0]
    first_token = place * tokens
    own = segment_ids.reshape(tokens, 1) + 1
    before = jnp.sum((marked < own).astype(jnp.int32), axis=1, keepdims=True)
    same = jnp.sum((earlier == own).astype(jnp.int32), axis=1, keepdims=True)
    starts = first_token + before - same
    query_index = first_token + jnp.arange(tokens, dtype=jnp.int32)[:, None]
    low = jnp.maximum(starts, query_index - (WIN - 1)) + jnp.zeros((1, HD), jnp.int32)
    steps = WIN // tokens // 2
    core = place % 2
    backs = [jnp.int32(2 * step) for step in range(steps + 1)]
    backs += [2 * step - 1 + 2 * core for step in range(steps + 1)]
    firsts = jnp.stack(backs) * -tokens + first_token
    meta = jnp.concatenate([first_token.reshape(1), firsts, firsts + half])
    later = 2 * (steps + 1)

    freqs = 10000.0 ** (-(jnp.arange(HD // 2, dtype=jnp.float32) * (2.0 / HD)))
    angles = (query_index - starts).astype(jnp.float32) * jnp.concatenate([freqs, freqs])[None, :]
    sign = np.where(np.arange(HD) < HD // 2, -1.0, 1.0).astype(np.float32)
    cos = jnp.cos(angles)
    sin = jnp.sin(angles) * sign[None, :]
    gain = norm_gain.reshape(1, -1)

    scale, q_part, k_part, v_part = project_early(
        shards, hidden, left, right, far_square, gain, w_query, w_key, w_value
    )
    normed, block, a0, b0, pages = project_kv(
        shards, table, far, scale, gain, w_key, w_value, k_part, v_part, cos, sin
    )

    def after(value, *others):
        return lax.optimization_barrier((value, *others))[0]

    def chain(name, block):
        arrived = [block]
        for step in range(1, steps + 1):
            with jax.named_scope(f"hop_{name}{step}"):
                arrived.append(shifted(arrived[-1], "seq", 2))
        return arrived

    def cross(name, block):
        with jax.named_scope(f"cross_{name}"):
            return swapped(block)

    a = chain("a", a0)
    b = chain("b", b0)
    look = functools.partial(attend, meta, low)
    straight = [1 + step for step in range(steps + 1)]
    over = [2 + steps + step for step in range(steps + 1)]
    queries = project_q(shards, normed, w_query, q_part, cos, sin)
    crossed = cross("own", after(block, queries))
    state = look(queries, [(block, straight[0], 0)])
    state = look(queries, [(crossed, over[0], None)], state, guarded=True)
    for step in range(1, steps):
        near, far = straight[step], over[step]
        parts = [
            (a[step], near, None),
            (cross(f"a{step}", a[step]), far, None),
            (b[step], near + later, None),
            (cross(f"b{step}", b[step]), far + later, None),
        ]
        state = look(queries, parts, state)
    kv_cache = exchange_pages(shards, after(pages, b[2]))
    near, far = straight[steps], over[steps]
    edge = [
        (cross(f"a{steps}", a[steps]), far, None),
        (cross(f"b{steps}", after(b[steps], *state, kv_cache)), far + later, None),
    ]
    state = look(queries, [(a[steps], near, None), (b[steps], near + later, None)], state)
    attended = look(queries, edge, state, last=True, guarded=True)
    return (attended, kv_cache)


def solution(mesh):
    placed = (
        P("seq", "tp"),
        P(),
        P(None, "tp"),
        P(None, "tp"),
        P(None, "tp"),
        P("seq"),
        P("seq", None),
    )
    return jax.shard_map(
        per_device,
        mesh=mesh,
        in_specs=placed,
        out_specs=(P("seq", "tp"), P(("seq", "tp"), None, None, None)),
        check_vma=False,
    )
```

```python
import functools

import jax
import jax.numpy as jnp
import numpy as np
from jax import lax
from jax.experimental import pallas as pl
from jax.experimental.pallas import tpu as pltpu
from jax.sharding import PartitionSpec as P

HD = 128
WIN = 4096
PAGE = 128
SPAN = 256

logit_cap = 50.0
query_scale = 144.0 ** (-0.5)
norm_eps = 1e-06
log2e = 1.4426950408889634

VMEM = pltpu.VMEM
SMEM = pltpu.SMEM


def whole(space=VMEM):
    return pl.BlockSpec(memory_space=space)


def shifted(block, axis, distance):
    devices = range(lax.axis_size(axis))
    route = [(i - distance, i) for i in devices if i - distance in devices]
    return lax.ppermute(block, axis, route)


def turned(block, axis, distance):
    count = lax.axis_size(axis)
    return lax.ppermute(block, axis, [(i, (i + distance) % count) for i in range(count)])


def swapped(block):
    return lax.ppermute(block, "seq", [(i, i ^ 1) for i in range(lax.axis_size("seq"))])


def rope(x, cos, sin):
    return x * cos + pltpu.roll(x, HD // 2, 1) * sin


def early_kernel(shards, own, left, right, far_square, gain, wq, wk, wv, *refs):
    scale_out, q_part, k_part, v_part, normed = refs
    rows, width = own.shape
    features = wk.shape[0]
    pieces = ((own, 0), (left, 3), (right, 1))

    for start in range(0, rows, 128):
        at = pl.ds(start, 128)
        square = jnp.zeros((128, HD), jnp.float32)
        for piece, turn in pieces:
            wide = piece[at, :].astype(jnp.float32)
            wide = wide * wide
            for lane in range(0, width, HD):
                square = square + wide[:, lane : lane + HD]
        square = jnp.sum(square, axis=-1, keepdims=True) + far_square[at, :1]
        scale = lax.rsqrt(square * (1.0 / features) + norm_eps)
        scale_out[at, :] = jnp.broadcast_to(scale, (128, HD))
        for index, (piece, turn) in enumerate(pieces):
            cols = pl.ds(pl.multiple_of(shards[turn] * width, 128), width)
            wide = piece[at, :].astype(jnp.float32)
            normed[index, at, :] = (wide * scale * gain[:, cols]).astype(jnp.bfloat16)
    for weights, out in ((wk, k_part), (wv, v_part), (wq, q_part)):
        total = 0.0
        for index, (piece, turn) in enumerate(pieces):
            at = pl.ds(pl.multiple_of(shards[turn] * width, 128), width)
            total = total + jnp.dot(
                normed[index], weights[at, :], preferred_element_type=jnp.float32
            )
        out[...] = total


def project_early(shards, own, left, right, far_square, gain, wq, wk, wv):
    rows, width = own.shape
    columns = (wq.shape[1], wk.shape[1], wv.shape[1])
    return pl.pallas_call(
        early_kernel,
        name="project_early",
        out_shape=tuple(
            jax.ShapeDtypeStruct((rows, n), jnp.float32) for n in (HD, *columns)
        ),
        in_specs=[whole(SMEM)] + [whole()] * 8,
        out_specs=(whole(),) * 4,
        scratch_shapes=(VMEM((3, rows, width), jnp.bfloat16),),
        compiler_params=pltpu.CompilerParams(vmem_limit_bytes=16 << 20),
        cost_estimate=pl.CostEstimate(
            flops=6 * rows * width * sum(columns),
            transcendentals=rows,
            bytes_accessed=6 * rows * width,
        ),
    )(shards, own, left, right, far_square, gain, wq, wk, wv)


def kv_kernel(shards, table, *refs):
    far_a, far_b, scale, gain, wk, wv, k_part, v_part, cos, sin = refs[:10]
    normed, block, first, second, pages = refs[10:]
    count = shards.shape[0]
    rows, width = normed.shape
    half = rows // 2
    mine = pl.ds(pl.multiple_of(shards[2] * width, 128), width)

    for start in range(0, rows, 128):
        at = pl.ds(start, 128)
        far = far_a if start < half else far_b
        wide = far[pl.ds(start % half, 128), :].astype(jnp.float32)
        normed[at, :] = (wide * scale[at, :1] * gain[:, mine]).astype(jnp.bfloat16)
    keys = k_part[...] + jnp.dot(normed[...], wk[mine, :], preferred_element_type=jnp.float32)
    values = v_part[...] + jnp.dot(normed[...], wv[mine, :], preferred_element_type=jnp.float32)
    kv_width = wk.shape[1]
    for out, start in ((first, 0), (second, half)):
        at = slice(start, start + half)
        for head in range(kv_width // HD):
            cols = slice(head * HD, head * HD + HD)
            out[:, cols] = rope(keys[at, cols], cos[at, :], sin[at, :]).astype(jnp.bfloat16)
        out[:, kv_width:] = values[at].astype(jnp.bfloat16)
        block[at, :] = out[...]
        for page in range(half // PAGE):
            slot = lax.rem(table[start // PAGE + page] - shards[0] + count, count)
            pages[slot, :, :] = out[page * PAGE : page * PAGE + PAGE, :]


def project_kv(shards, table, far, scale, gain, wk, wv, k_part, v_part, cos, sin):
    rows = cos.shape[0]
    far_width = far[0].shape[1]
    width = 2 * wk.shape[1]
    shapes = ((rows, far_width), (rows, width), (rows // 2, width), (rows // 2, width))
    shapes += ((rows // PAGE, PAGE, width),)
    return pl.pallas_call(
        kv_kernel,
        name="project_kv",
        out_shape=tuple(jax.ShapeDtypeStruct(shape, jnp.bfloat16) for shape in shapes),
        in_specs=[whole(SMEM)] * 2 + [whole()] * 10,
        out_specs=(whole(),) * 5,
        compiler_params=pltpu.CompilerParams(vmem_limit_bytes=10 << 20),
        cost_estimate=pl.CostEstimate(
            flops=2 * rows * far_width * width,
            transcendentals=0,
            bytes_accessed=2 * rows * far_width,
        ),
    )(shards, table, *far, scale, gain, wk, wv, k_part, v_part, cos, sin)


def q_kernel(shards, normed, wq, part, cos, sin, out):
    width = normed.shape[1]
    mine = pl.ds(pl.multiple_of(shards[2] * width, 128), width)
    raw = part[...] + jnp.dot(normed[...], wq[mine, :], preferred_element_type=jnp.float32)
    for head in range(wq.shape[1] // HD):
        cols = slice(head * HD, head * HD + HD)
        out[:, cols] = rope(raw[:, cols], cos[...], sin[...]).astype(jnp.bfloat16)


def project_q(shards, normed, wq, part, cos, sin):
    rows, width = part.shape
    return pl.pallas_call(
        q_kernel,
        name="project_q",
        out_shape=jax.ShapeDtypeStruct((rows, width), jnp.bfloat16),
        in_specs=[whole(SMEM)] + [whole()] * 5,
        out_specs=whole(),
        compiler_params=pltpu.CompilerParams(vmem_limit_bytes=8 << 20),
        cost_estimate=pl.CostEstimate(
            flops=1000000 * rows, transcendentals=0, bytes_accessed=rows * width
        ),
    )(shards, normed, wq, part, cos, sin)


def attend_kernel(places, first, last, guarded, meta, low_ref, q_ref, *refs):
    count = len(places)
    blocks = refs[:count]
    refs = refs[count:]
    if first:
        acc, tot = refs[-2:]
        acc[...] = jnp.zeros_like(acc)
        tot[...] = jnp.zeros_like(tot)
    else:
        acc_in, tot_in = refs[:2]
        if last:
            out, acc, tot = refs[2:]
            acc[...] = acc_in[...]
            tot[...] = tot_in[...]
        else:
            acc, tot = refs[2:]
    rows = q_ref.shape[0]
    heads = q_ref.shape[1] // HD
    kv_width = blocks[0].shape[1] // 2
    repeat = heads * HD // kv_width

    def visit(block, index, base, top):
        span = SPAN
        key_first = meta[index] + base
        at = slice(top or 0, rows)
        here = (at.stop - at.start, span)
        key_index = key_first + lax.broadcasted_iota(jnp.int32, here, 1)
        allowed = key_index >= jnp.concatenate([low_ref[at, :]] * (span // HD), axis=1)
        if top is not None:
            row = meta[0] + top + lax.broadcasted_iota(jnp.int32, here, 0)
            allowed = allowed & (key_index <= row)
        for head in range(heads):
            cols = slice(head * HD, head * HD + HD)
            group = head // repeat
            keys = block[base : base + span, group * HD : group * HD + HD]
            values = block[
                base : base + span, kv_width + group * HD : kv_width + group * HD + HD
            ]
            raw = lax.dot_general(
                q_ref[at, cols],
                keys,
                (((1,), (1,)), ((), ())),
                preferred_element_type=jnp.float32,
            )
            capped = jnp.tanh(raw * (query_scale / logit_cap))
            weights = jnp.where(allowed, jnp.exp2(capped * (logit_cap * log2e)), 0.0)
            part = weights[:, :HD]
            for k in range(HD, span, HD):
                part = part + weights[:, k : k + HD]
            tot[at, cols] += part
            acc[at, cols] += jnp.dot(
                weights.astype(jnp.bfloat16), values, preferred_element_type=jnp.float32
            )

    def visit_all():
        for block, (index, top) in zip(blocks, places):
            for base in range(0, block.shape[0], SPAN):
                visit(block, index, base, None if top is None else top + base)

    if guarded:
        key_first = meta[places[0][0]]
        pl.when((key_first <= meta[0]) & (key_first + rows > meta[0] - WIN))(visit_all)
    else:
        visit_all()
    if last:
        for head in range(heads):
            cols = slice(head * HD, head * HD + HD)
            total = jnp.sum(tot[:, cols], axis=-1, keepdims=True)
            out[:, cols] = (acc[:, cols] / total).astype(jnp.bfloat16)


def attend(meta, low, queries, parts, state=None, last=False, guarded=False):
    rows, width = queries.shape
    places = tuple((index, top) for _, index, top in parts)
    blocks = [block for block, _, _ in parts]
    wide = jax.ShapeDtypeStruct((rows, width), jnp.float32)
    first = state is None
    operands = [meta, low, queries, *blocks] + ([] if first else list(state))
    keys = sum(block.shape[0] for block in blocks)
    scratch = ()
    aliases = {}
    if last:
        out_shape = jax.ShapeDtypeStruct((rows, width), jnp.bfloat16)
        out_specs = whole()
        scratch = (VMEM((rows, width), jnp.float32), VMEM((rows, width), jnp.float32))
    else:
        out_shape = (wide, wide)
        out_specs = (whole(), whole())
        if not first:
            aliases = {len(operands) - 2: 0, len(operands) - 1: 1}
    return pl.pallas_call(
        functools.partial(attend_kernel, places, first, last, guarded),
        name="attend_last" if last else "attend",
        out_shape=out_shape,
        in_specs=[whole(SMEM)] + [whole()] * (len(operands) - 1),
        out_specs=out_specs,
        scratch_shapes=scratch,
        input_output_aliases=aliases,
        compiler_params=pltpu.CompilerParams(vmem_limit_bytes=8 << 20),
        cost_estimate=pl.CostEstimate(
            flops=2000000 * keys,
            transcendentals=0,
            bytes_accessed=width * keys,
        ),
    )(*operands)


def cache_kernel(shards, *refs):
    out = refs[-1]
    count = len(refs) - 1
    width = refs[0].shape[1] // 2
    for turn, received in enumerate(refs[:-1]):
        shard = shards[(count - turn) % count]
        cols = pl.ds(pl.multiple_of(shard * width, 128), width)
        for index in range(2):
            out[0, :, index, cols] = received[:, index * width : index * width + width]


def exchange_pages(shards, pages):
    count, rows, width = pages.shape
    received = [pages[0]]
    for turn in range(1, count):
        received.append(turned(pages[turn], "tp", turn))
    return pl.pallas_call(
        cache_kernel,
        name="build_cache",
        out_shape=jax.ShapeDtypeStruct((1, rows, 2, count * width // 2), pages.dtype),
        in_specs=[whole(SMEM)] + [whole()] * count,
        out_specs=whole(),
        compiler_params=pltpu.CompilerParams(vmem_limit_bytes=8 << 20),
        cost_estimate=pl.CostEstimate(flops=1000000000, transcendentals=0, bytes_accessed=1000),
    )(shards, *received)


def halves_kernel(left, right, left_out, right_out):
    half = left_out.shape[0]
    left_out[...] = left[:half, :]
    right_out[...] = right[half:, :]


def halves(left, right):
    rows, width = left.shape
    half = jax.ShapeDtypeStruct((rows // 2, width), left.dtype)
    return pl.pallas_call(
        halves_kernel,
        name="halves",
        out_shape=(half, half),
        in_specs=[whole()] * 2,
        out_specs=(whole(), whole()),
        compiler_params=pltpu.CompilerParams(vmem_limit_bytes=8 << 20),
        cost_estimate=pl.CostEstimate(flops=20000000000, transcendentals=0, bytes_accessed=4 * rows * width),
    )(left, right)


def ring_gather(block):
    rows = block.shape[0]
    half = rows // 2
    left = turned(block, "tp", 1)
    right = turned(block, "tp", -1)
    left_half, right_half = halves(left, right)
    far_a = turned(left_half, "tp", 1)
    far_b = turned(right_half, "tp", -1)
    return left, right, (far_a, far_b), left_half


def per_device(hidden, norm_gain, w_query, w_key, w_value, segment_ids, page_table):
    tokens = hidden.shape[0]
    place = lax.axis_index("seq")
    rank = lax.axis_index("tp")
    half = tokens // 2
    ranks = lax.axis_size("tp")
    shards = (rank + jnp.arange(ranks, dtype=jnp.int32)) % ranks
    table = page_table[0]

    left, right, far, forwarded = ring_gather(hidden)
    wide = hidden.astype(jnp.float32)
    with jax.named_scope("far_square"):
        far_square = turned(jnp.sum(wide * wide, axis=-1).reshape(1, tokens), "tp", 2)
    far_square = far_square.reshape(tokens, 1) + jnp.zeros((1, HD), jnp.float32)
    first_token = place * tokens
    steps = WIN // tokens // 2
    core = place % 2
    backs = [jnp.int32(2 * step) for step in range(steps + 1)]
    backs += [2 * step - 1 + 2 * core for step in range(steps + 1)]
    firsts = jnp.stack(backs) * -tokens + first_token
    meta = jnp.concatenate([first_token.reshape(1), firsts, firsts + half])
    later = 2 * (steps + 1)
    marked = (segment_ids + 1).reshape(1, tokens)
    marked, meta = lax.optimization_barrier((marked, meta))
    near = jnp.concatenate(
        [marked, shifted(marked, "seq", 1), shifted(marked, "seq", 2)], axis=0
    )
    earlier = jnp.concatenate(
        [near[1:], shifted(near, "seq", 3), shifted(near, "seq", 6)], axis=0
    ).reshape(1, -1)
    earlier = lax.optimization_barrier((earlier, forwarded))[0]
    own = segment_ids.reshape(tokens, 1) + 1
    before = jnp.sum((marked < own).astype(jnp.int32), axis=1, keepdims=True)
    same = jnp.sum((earlier == own).astype(jnp.int32), axis=1, keepdims=True)
    starts = first_token + before - same
    query_index = first_token + jnp.arange(tokens, dtype=jnp.int32)[:, None]
    low = jnp.maximum(starts, query_index - (WIN - 1)) + jnp.zeros((1, HD), jnp.int32)
    freqs = 10000.0 ** (-(jnp.arange(HD // 2, dtype=jnp.float32) * (2.0 / HD)))
    angles = (query_index - starts).astype(jnp.float32) * jnp.concatenate([freqs, freqs])[None, :]
    sign = np.where(np.arange(HD) < HD // 2, -1.0, 1.0).astype(np.float32)
    cos = jnp.cos(angles)
    sin = jnp.sin(angles) * sign[None, :]
    gain = norm_gain.reshape(1, -1)

    scale, q_part, k_part, v_part = project_early(
        shards, hidden, left, right, far_square, gain, w_query, w_key, w_value
    )
    normed, block, a0, b0, pages = project_kv(
        shards, table, far, scale, gain, w_key, w_value, k_part, v_part, cos, sin
    )

    def after(value, *others):
        return lax.optimization_barrier((value, *others))[0]

    def chain(name, block, ahead):
        arrived = [block]
        for step in range(1, steps + 1):
            moving = after(arrived[-1], ahead) if step == 2 else arrived[-1]
            with jax.named_scope(f"hop_{name}{step}"):
                arrived.append(shifted(moving, "seq", 2))
        return arrived

    def cross(name, block):
        with jax.named_scope(f"cross_{name}"):
            return swapped(block)

    queries = project_q(shards, normed, w_query, q_part, cos, sin)
    a = chain("a", a0, queries)
    b = chain("b", b0, queries)
    look = functools.partial(attend, meta, low)
    straight = [1 + step for step in range(steps + 1)]
    over = [2 + steps + step for step in range(steps + 1)]
    crossed = cross("own", after(block, queries))
    state = look(queries, [(block, straight[0], 0)])
    state = look(queries, [(crossed, over[0], None)], state, guarded=True)
    for step in range(1, steps):
        near, far = straight[step], over[step]
        parts = [
            (a[step], near, None),
            (cross(f"a{step}", a[step]), far, None),
            (b[step], near + later, None),
            (cross(f"b{step}", b[step]), far + later, None),
        ]
        state = look(queries, parts, state)
    kv_cache = exchange_pages(shards, after(pages, b[2]))
    near, far = straight[steps], over[steps]
    edge = [
        (cross(f"a{steps}", a[steps]), far, None),
        (cross(f"b{steps}", after(b[steps], *state, kv_cache)), far + later, None),
    ]
    state = look(queries, [(a[steps], near, None), (b[steps], near + later, None)], state)
    attended = look(queries, edge, state, last=True, guarded=True)
    return (attended, kv_cache)


def solution(mesh):
    placed = (
        P("seq", "tp"),
        P(),
        P(None, "tp"),
        P(None, "tp"),
        P(None, "tp"),
        P("seq"),
        P("seq", None),
    )
    return jax.shard_map(
        per_device,
        mesh=mesh,
        in_specs=placed,
        out_specs=(P("seq", "tp"), P(("seq", "tp"), None, None, None)),
        check_vma=False,
    )
```

```python
import functools

import jax
import jax.numpy as jnp
import numpy as np
from jax import lax
from jax.experimental import pallas as pl
from jax.experimental.pallas import tpu as pltpu
from jax.sharding import PartitionSpec as P

HD = 128
WIN = 4096
PAGE = 128
SPAN = 256

logit_cap = 50.0
query_scale = 144.0 ** (-0.5)
norm_eps = 1e-06
log2e = 1.4426950408889634

VMEM = pltpu.VMEM
SMEM = pltpu.SMEM


def whole(space=VMEM):
    return pl.BlockSpec(memory_space=space)


def shifted(block, axis, distance):
    devices = range(lax.axis_size(axis))
    route = [(i - distance, i) for i in devices if i - distance in devices]
    return lax.ppermute(block, axis, route)


def turned(block, axis, distance):
    count = lax.axis_size(axis)
    return lax.ppermute(block, axis, [(i, (i + distance) % count) for i in range(count)])


def swapped(block):
    return lax.ppermute(block, "seq", [(i, i ^ 1) for i in range(lax.axis_size("seq"))])


def rope(x, cos, sin):
    return x * cos + pltpu.roll(x, HD // 2, 1) * sin


def early_kernel(shards, own, left, right, far_square, gain, wq, wk, wv, *refs):
    scale_out, q_part, k_part, v_part, normed = refs
    rows, width = own.shape
    features = wk.shape[0]
    pieces = ((own, 0), (left, 3), (right, 1))

    for start in range(0, rows, 128):
        at = pl.ds(start, 128)
        square = jnp.zeros((128, HD), jnp.float32)
        for piece, turn in pieces:
            wide = piece[at, :].astype(jnp.float32)
            wide = wide * wide
            for lane in range(0, width, HD):
                square = square + wide[:, lane : lane + HD]
        square = jnp.sum(square, axis=-1, keepdims=True) + far_square[at, :1]
        scale = lax.rsqrt(square * (1.0 / features) + norm_eps)
        scale_out[at, :] = jnp.broadcast_to(scale, (128, HD))
        for index, (piece, turn) in enumerate(pieces):
            cols = pl.ds(pl.multiple_of(shards[turn] * width, 128), width)
            wide = piece[at, :].astype(jnp.float32)
            normed[index, at, :] = (wide * scale * gain[:, cols]).astype(jnp.bfloat16)
    for weights, out in ((wk, k_part), (wv, v_part), (wq, q_part)):
        total = 0.0
        for index, (piece, turn) in enumerate(pieces):
            at = pl.ds(pl.multiple_of(shards[turn] * width, 128), width)
            total = total + jnp.dot(
                normed[index], weights[at, :], preferred_element_type=jnp.float32
            )
        out[...] = total


def project_early(shards, own, left, right, far_square, gain, wq, wk, wv):
    rows, width = own.shape
    columns = (wq.shape[1], wk.shape[1], wv.shape[1])
    return pl.pallas_call(
        early_kernel,
        name="project_early",
        out_shape=tuple(
            jax.ShapeDtypeStruct((rows, n), jnp.float32) for n in (HD, *columns)
        ),
        in_specs=[whole(SMEM)] + [whole()] * 8,
        out_specs=(whole(),) * 4,
        scratch_shapes=(VMEM((3, rows, width), jnp.bfloat16),),
        compiler_params=pltpu.CompilerParams(vmem_limit_bytes=16 << 20),
        cost_estimate=pl.CostEstimate(
            flops=6 * rows * width * sum(columns),
            transcendentals=rows,
            bytes_accessed=6 * rows * width,
        ),
    )(shards, own, left, right, far_square, gain, wq, wk, wv)


def kv_kernel(shards, table, *refs):
    far_a, far_b, scale, gain, wk, wv, k_part, v_part, cos, sin = refs[:10]
    normed, block, first, second, pages = refs[10:]
    count = shards.shape[0]
    rows, width = normed.shape
    half = rows // 2
    mine = pl.ds(pl.multiple_of(shards[2] * width, 128), width)

    for start in range(0, rows, 128):
        at = pl.ds(start, 128)
        far = far_a if start < half else far_b
        wide = far[pl.ds(start % half, 128), :].astype(jnp.float32)
        normed[at, :] = (wide * scale[at, :1] * gain[:, mine]).astype(jnp.bfloat16)
    keys = k_part[...] + jnp.dot(normed[...], wk[mine, :], preferred_element_type=jnp.float32)
    values = v_part[...] + jnp.dot(normed[...], wv[mine, :], preferred_element_type=jnp.float32)
    kv_width = wk.shape[1]
    for out, start in ((first, 0), (second, half)):
        at = slice(start, start + half)
        for head in range(kv_width // HD):
            cols = slice(head * HD, head * HD + HD)
            out[:, cols] = rope(keys[at, cols], cos[at, :], sin[at, :]).astype(jnp.bfloat16)
        out[:, kv_width:] = values[at].astype(jnp.bfloat16)
        block[at, :] = out[...]
        for page in range(half // PAGE):
            slot = lax.rem(table[start // PAGE + page] - shards[0] + count, count)
            pages[slot, :, :] = out[page * PAGE : page * PAGE + PAGE, :]


def project_kv(shards, table, far, scale, gain, wk, wv, k_part, v_part, cos, sin):
    rows = cos.shape[0]
    far_width = far[0].shape[1]
    width = 2 * wk.shape[1]
    shapes = ((rows, far_width), (rows, width), (rows // 2, width), (rows // 2, width))
    shapes += ((rows // PAGE, PAGE, width),)
    return pl.pallas_call(
        kv_kernel,
        name="project_kv",
        out_shape=tuple(jax.ShapeDtypeStruct(shape, jnp.bfloat16) for shape in shapes),
        in_specs=[whole(SMEM)] * 2 + [whole()] * 10,
        out_specs=(whole(),) * 5,
        compiler_params=pltpu.CompilerParams(vmem_limit_bytes=10 << 20),
        cost_estimate=pl.CostEstimate(
            flops=2 * rows * far_width * width,
            transcendentals=0,
            bytes_accessed=2 * rows * far_width,
        ),
    )(shards, table, *far, scale, gain, wk, wv, k_part, v_part, cos, sin)


def q_kernel(shards, normed, wq, part, cos, sin, out):
    width = normed.shape[1]
    mine = pl.ds(pl.multiple_of(shards[2] * width, 128), width)
    raw = part[...] + jnp.dot(normed[...], wq[mine, :], preferred_element_type=jnp.float32)
    for head in range(wq.shape[1] // HD):
        cols = slice(head * HD, head * HD + HD)
        out[:, cols] = rope(raw[:, cols], cos[...], sin[...]).astype(jnp.bfloat16)


def project_q(shards, normed, wq, part, cos, sin):
    rows, width = part.shape
    return pl.pallas_call(
        q_kernel,
        name="project_q",
        out_shape=jax.ShapeDtypeStruct((rows, width), jnp.bfloat16),
        in_specs=[whole(SMEM)] + [whole()] * 5,
        out_specs=whole(),
        compiler_params=pltpu.CompilerParams(vmem_limit_bytes=8 << 20),
        cost_estimate=pl.CostEstimate(
            flops=10000000 * rows, transcendentals=0, bytes_accessed=rows * width
        ),
    )(shards, normed, wq, part, cos, sin)


def attend_kernel(places, first, last, guarded, meta, low_ref, q_ref, *refs):
    count = len(places)
    blocks = refs[:count]
    refs = refs[count:]
    if first:
        acc, tot = refs[-2:]
        acc[...] = jnp.zeros_like(acc)
        tot[...] = jnp.zeros_like(tot)
    else:
        acc_in, tot_in = refs[:2]
        if last:
            out, acc, tot = refs[2:]
            acc[...] = acc_in[...]
            tot[...] = tot_in[...]
        else:
            acc, tot = refs[2:]
    rows = q_ref.shape[0]
    heads = q_ref.shape[1] // HD
    kv_width = blocks[0].shape[1] // 2
    repeat = heads * HD // kv_width

    def visit(block, index, base, top):
        span = SPAN
        key_first = meta[index] + base
        at = slice(top or 0, rows)
        here = (at.stop - at.start, span)
        key_index = key_first + lax.broadcasted_iota(jnp.int32, here, 1)
        allowed = key_index >= jnp.concatenate([low_ref[at, :]] * (span // HD), axis=1)
        if top is not None:
            row = meta[0] + top + lax.broadcasted_iota(jnp.int32, here, 0)
            allowed = allowed & (key_index <= row)
        for head in range(heads):
            cols = slice(head * HD, head * HD + HD)
            group = head // repeat
            keys = block[base : base + span, group * HD : group * HD + HD]
            values = block[
                base : base + span, kv_width + group * HD : kv_width + group * HD + HD
            ]
            raw = lax.dot_general(
                q_ref[at, cols],
                keys,
                (((1,), (1,)), ((), ())),
                preferred_element_type=jnp.float32,
            )
            capped = jnp.tanh(raw * (query_scale / logit_cap))
            weights = jnp.where(allowed, jnp.exp2(capped * (logit_cap * log2e)), 0.0)
            part = weights[:, :HD]
            for k in range(HD, span, HD):
                part = part + weights[:, k : k + HD]
            tot[at, cols] += part
            acc[at, cols] += jnp.dot(
                weights.astype(jnp.bfloat16), values, preferred_element_type=jnp.float32
            )

    def visit_all():
        for block, (index, top) in zip(blocks, places):
            for base in range(0, block.shape[0], SPAN):
                visit(block, index, base, None if top is None else top + base)

    if guarded:
        key_first = meta[places[0][0]]
        pl.when((key_first <= meta[0]) & (key_first + rows > meta[0] - WIN))(visit_all)
    else:
        visit_all()
    if last:
        for head in range(heads):
            cols = slice(head * HD, head * HD + HD)
            total = jnp.sum(tot[:, cols], axis=-1, keepdims=True)
            out[:, cols] = (acc[:, cols] / total).astype(jnp.bfloat16)


def attend(meta, low, queries, parts, state=None, last=False, guarded=False):
    rows, width = queries.shape
    places = tuple((index, top) for _, index, top in parts)
    blocks = [block for block, _, _ in parts]
    wide = jax.ShapeDtypeStruct((rows, width), jnp.float32)
    first = state is None
    operands = [meta, low, queries, *blocks] + ([] if first else list(state))
    keys = sum(block.shape[0] for block in blocks)
    scratch = ()
    aliases = {}
    if last:
        out_shape = jax.ShapeDtypeStruct((rows, width), jnp.bfloat16)
        out_specs = whole()
        scratch = (VMEM((rows, width), jnp.float32), VMEM((rows, width), jnp.float32))
    else:
        out_shape = (wide, wide)
        out_specs = (whole(), whole())
        if not first:
            aliases = {len(operands) - 2: 0, len(operands) - 1: 1}
    return pl.pallas_call(
        functools.partial(attend_kernel, places, first, last, guarded),
        name="attend_last" if last else "attend",
        out_shape=out_shape,
        in_specs=[whole(SMEM)] + [whole()] * (len(operands) - 1),
        out_specs=out_specs,
        scratch_shapes=scratch,
        input_output_aliases=aliases,
        compiler_params=pltpu.CompilerParams(vmem_limit_bytes=8 << 20),
        cost_estimate=pl.CostEstimate(
            flops=10000000 * keys,
            transcendentals=0,
            bytes_accessed=width * keys,
        ),
    )(*operands)


def cache_kernel(shards, *refs):
    out = refs[-1]
    count = len(refs) - 1
    width = refs[0].shape[1] // 2
    for turn, received in enumerate(refs[:-1]):
        shard = shards[(count - turn) % count]
        cols = pl.ds(pl.multiple_of(shard * width, 128), width)
        for index in range(2):
            out[0, :, index, cols] = received[:, index * width : index * width + width]


def exchange_pages(shards, pages):
    count, rows, width = pages.shape
    received = [pages[0]]
    for turn in range(1, count):
        received.append(turned(pages[turn], "tp", turn))
    return pl.pallas_call(
        cache_kernel,
        name="build_cache",
        out_shape=jax.ShapeDtypeStruct((1, rows, 2, count * width // 2), pages.dtype),
        in_specs=[whole(SMEM)] + [whole()] * count,
        out_specs=whole(),
        compiler_params=pltpu.CompilerParams(vmem_limit_bytes=8 << 20),
        cost_estimate=pl.CostEstimate(flops=1000000000, transcendentals=0, bytes_accessed=1000),
    )(shards, *received)


def halves_kernel(left, right, left_out, right_out):
    half = left_out.shape[0]
    left_out[...] = left[:half, :]
    right_out[...] = right[half:, :]


def halves(left, right):
    rows, width = left.shape
    half = jax.ShapeDtypeStruct((rows // 2, width), left.dtype)
    return pl.pallas_call(
        halves_kernel,
        name="halves",
        out_shape=(half, half),
        in_specs=[whole()] * 2,
        out_specs=(whole(), whole()),
        compiler_params=pltpu.CompilerParams(vmem_limit_bytes=8 << 20),
        cost_estimate=pl.CostEstimate(flops=20000000000, transcendentals=0, bytes_accessed=4 * rows * width),
    )(left, right)


def ring_gather(block):
    rows = block.shape[0]
    half = rows // 2
    left = turned(block, "tp", 1)
    right = turned(block, "tp", -1)
    left_half, right_half = halves(left, right)
    far_a = turned(left_half, "tp", 1)
    far_b = turned(right_half, "tp", -1)
    return left, right, (far_a, far_b), left_half


def per_device(hidden, norm_gain, w_query, w_key, w_value, segment_ids, page_table):
    tokens = hidden.shape[0]
    place = lax.axis_index("seq")
    rank = lax.axis_index("tp")
    half = tokens // 2
    ranks = lax.axis_size("tp")
    shards = (rank + jnp.arange(ranks, dtype=jnp.int32)) % ranks
    table = page_table[0]

    left, right, far, forwarded = ring_gather(hidden)
    wide = hidden.astype(jnp.float32)
    with jax.named_scope("far_square"):
        far_square = turned(jnp.sum(wide * wide, axis=-1).reshape(1, tokens), "tp", 2)
    far_square = far_square.reshape(tokens, 1) + jnp.zeros((1, HD), jnp.float32)
    marked = (segment_ids + 1).reshape(1, tokens)
    near = jnp.concatenate(
        [marked, shifted(marked, "seq", 1), shifted(marked, "seq", 2)], axis=0
    )
    earlier = jnp.concatenate(
        [near[1:], shifted(near, "seq", 3), shifted(near, "seq", 6)], axis=0
    ).reshape(1, -1)
    earlier = lax.optimization_barrier((earlier, forwarded))[0]
    first_token = place * tokens
    own = segment_ids.reshape(tokens, 1) + 1
    before = jnp.sum((marked < own).astype(jnp.int32), axis=1, keepdims=True)
    same = jnp.sum((earlier == own).astype(jnp.int32), axis=1, keepdims=True)
    starts = first_token + before - same
    query_index = first_token + jnp.arange(tokens, dtype=jnp.int32)[:, None]
    low = jnp.maximum(starts, query_index - (WIN - 1)) + jnp.zeros((1, HD), jnp.int32)
    steps = WIN // tokens // 2
    core = place % 2
    backs = [jnp.int32(2 * step) for step in range(steps + 1)]
    backs += [2 * step - 1 + 2 * core for step in range(steps + 1)]
    firsts = jnp.stack(backs) * -tokens + first_token
    meta = jnp.concatenate([first_token.reshape(1), firsts, firsts + half])
    later = 2 * (steps + 1)

    freqs = 10000.0 ** (-(jnp.arange(HD // 2, dtype=jnp.float32) * (2.0 / HD)))
    angles = (query_index - starts).astype(jnp.float32) * jnp.concatenate([freqs, freqs])[None, :]
    sign = np.where(np.arange(HD) < HD // 2, -1.0, 1.0).astype(np.float32)
    cos = jnp.cos(angles)
    sin = jnp.sin(angles) * sign[None, :]
    gain = norm_gain.reshape(1, -1)

    scale, q_part, k_part, v_part = project_early(
        shards, hidden, left, right, far_square, gain, w_query, w_key, w_value
    )
    normed, block, a0, b0, pages = project_kv(
        shards, table, far, scale, gain, w_key, w_value, k_part, v_part, cos, sin
    )

    def after(value, *others):
        return lax.optimization_barrier((value, *others))[0]

    def hop(name, block, distance):
        with jax.named_scope(f"hop_{name}"):
            return shifted(block, "seq", distance)

    def cross(name, block):
        with jax.named_scope(f"cross_{name}"):
            return swapped(block)

    arrived = [block]
    for step in range(1, steps):
        arrived.append(hop(step, arrived[-1], 2))
    arrived.append(hop("direct", block, 2 * steps))
    look = functools.partial(attend, meta, low)
    straight = [1 + step for step in range(steps + 1)]
    over = [2 + steps + step for step in range(steps + 1)]
    queries = project_q(shards, normed, w_query, q_part, cos, sin)
    crossed = cross("own", after(block, queries))
    state = look(queries, [(block, straight[0], 0)])
    state = look(queries, [(crossed, over[0], None)], state, guarded=True)
    kv_cache = exchange_pages(shards, after(pages, arrived[1]))
    for step in range(1, steps - 1):
        crossed = cross(step, arrived[step])
        state = look(queries, [(arrived[step], straight[step], None)], state)
        if step == steps - 2:
            far_block = after(arrived[steps], *state)
        state = look(queries, [(crossed, over[step], None)], state)
    crossed = cross(steps, far_block)
    state = look(queries, [(far_block, straight[steps], None)], state)
    state = look(queries, [(crossed, over[steps], None)], state, guarded=True)
    crossed = cross(steps - 1, after(arrived[steps - 1], kv_cache))
    state = look(queries, [(arrived[steps - 1], straight[steps - 1], None)], state)
    attended = look(queries, [(crossed, over[steps - 1], None)], state, last=True)
    return (attended, kv_cache)


def solution(mesh):
    placed = (
        P("seq", "tp"),
        P(),
        P(None, "tp"),
        P(None, "tp"),
        P(None, "tp"),
        P("seq"),
        P("seq", None),
    )
    return jax.shard_map(
        per_device,
        mesh=mesh,
        in_specs=placed,
        out_specs=(P("seq", "tp"), P(("seq", "tp"), None, None, None)),
        check_vma=False,
    )
```

```python
import functools

import jax
import jax.numpy as jnp
import numpy as np
from jax import lax
from jax.experimental import pallas as pl
from jax.experimental.pallas import tpu as pltpu
from jax.sharding import PartitionSpec as P

HD = 128
WIN = 4096
PAGE = 128
SPAN = 256

logit_cap = 50.0
query_scale = 144.0 ** (-0.5)
norm_eps = 1e-06
log2e = 1.4426950408889634

VMEM = pltpu.VMEM
SMEM = pltpu.SMEM


def whole(space=VMEM):
    return pl.BlockSpec(memory_space=space)


def shifted(block, axis, distance):
    devices = range(lax.axis_size(axis))
    route = [(i - distance, i) for i in devices if i - distance in devices]
    return lax.ppermute(block, axis, route)


def turned(block, axis, distance):
    count = lax.axis_size(axis)
    return lax.ppermute(block, axis, [(i, (i + distance) % count) for i in range(count)])


def swapped(block):
    return lax.ppermute(block, "seq", [(i, i ^ 1) for i in range(lax.axis_size("seq"))])


def rope(x, cos, sin):
    return x * cos + pltpu.roll(x, HD // 2, 1) * sin


def early_kernel(shards, own, left, right, far_square, gain, wq, wk, wv, *refs):
    scale_out, q_part, k_part, v_part, normed = refs
    rows, width = own.shape
    features = wk.shape[0]
    pieces = ((own, 0), (left, 3), (right, 1))

    for start in range(0, rows, 128):
        at = pl.ds(start, 128)
        square = jnp.zeros((128, HD), jnp.float32)
        for piece, turn in pieces:
            wide = piece[at, :].astype(jnp.float32)
            wide = wide * wide
            for lane in range(0, width, HD):
                square = square + wide[:, lane : lane + HD]
        square = jnp.sum(square, axis=-1, keepdims=True) + far_square[at, :1]
        scale = lax.rsqrt(square * (1.0 / features) + norm_eps)
        scale_out[at, :] = jnp.broadcast_to(scale, (128, HD))
        for index, (piece, turn) in enumerate(pieces):
            cols = pl.ds(pl.multiple_of(shards[turn] * width, 128), width)
            wide = piece[at, :].astype(jnp.float32)
            normed[index, at, :] = (wide * scale * gain[:, cols]).astype(jnp.bfloat16)
    for weights, out in ((wk, k_part), (wv, v_part), (wq, q_part)):
        total = 0.0
        for index, (piece, turn) in enumerate(pieces):
            at = pl.ds(pl.multiple_of(shards[turn] * width, 128), width)
            total = total + jnp.dot(
                normed[index], weights[at, :], preferred_element_type=jnp.float32
            )
        out[...] = total


def project_early(shards, own, left, right, far_square, gain, wq, wk, wv):
    rows, width = own.shape
    columns = (wq.shape[1], wk.shape[1], wv.shape[1])
    return pl.pallas_call(
        early_kernel,
        name="project_early",
        out_shape=tuple(
            jax.ShapeDtypeStruct((rows, n), jnp.float32) for n in (HD, *columns)
        ),
        in_specs=[whole(SMEM)] + [whole()] * 8,
        out_specs=(whole(),) * 4,
        scratch_shapes=(VMEM((3, rows, width), jnp.bfloat16),),
        compiler_params=pltpu.CompilerParams(vmem_limit_bytes=16 << 20),
        cost_estimate=pl.CostEstimate(
            flops=6 * rows * width * sum(columns),
            transcendentals=rows,
            bytes_accessed=6 * rows * width,
        ),
    )(shards, own, left, right, far_square, gain, wq, wk, wv)


def kv_kernel(shards, table, *refs):
    far_a, far_b, scale, gain, wk, wv, k_part, v_part, cos, sin = refs[:10]
    normed, block, first, second, pages = refs[10:]
    count = shards.shape[0]
    rows, width = normed.shape
    half = rows // 2
    mine = pl.ds(pl.multiple_of(shards[2] * width, 128), width)

    for start in range(0, rows, 128):
        at = pl.ds(start, 128)
        far = far_a if start < half else far_b
        wide = far[pl.ds(start % half, 128), :].astype(jnp.float32)
        normed[at, :] = (wide * scale[at, :1] * gain[:, mine]).astype(jnp.bfloat16)
    keys = k_part[...] + jnp.dot(normed[...], wk[mine, :], preferred_element_type=jnp.float32)
    values = v_part[...] + jnp.dot(normed[...], wv[mine, :], preferred_element_type=jnp.float32)
    kv_width = wk.shape[1]
    for out, start in ((first, 0), (second, half)):
        at = slice(start, start + half)
        for head in range(kv_width // HD):
            cols = slice(head * HD, head * HD + HD)
            out[:, cols] = rope(keys[at, cols], cos[at, :], sin[at, :]).astype(jnp.bfloat16)
        out[:, kv_width:] = values[at].astype(jnp.bfloat16)
        block[at, :] = out[...]
        for page in range(half // PAGE):
            slot = lax.rem(table[start // PAGE + page] - shards[0] + count, count)
            pages[slot, :, :] = out[page * PAGE : page * PAGE + PAGE, :]


def project_kv(shards, table, far, scale, gain, wk, wv, k_part, v_part, cos, sin):
    rows = cos.shape[0]
    far_width = far[0].shape[1]
    width = 2 * wk.shape[1]
    shapes = ((rows, far_width), (rows, width), (rows // 2, width), (rows // 2, width))
    shapes += ((rows // PAGE, PAGE, width),)
    return pl.pallas_call(
        kv_kernel,
        name="project_kv",
        out_shape=tuple(jax.ShapeDtypeStruct(shape, jnp.bfloat16) for shape in shapes),
        in_specs=[whole(SMEM)] * 2 + [whole()] * 10,
        out_specs=(whole(),) * 5,
        compiler_params=pltpu.CompilerParams(vmem_limit_bytes=10 << 20),
        cost_estimate=pl.CostEstimate(
            flops=2 * rows * far_width * width,
            transcendentals=0,
            bytes_accessed=2 * rows * far_width,
        ),
    )(shards, table, *far, scale, gain, wk, wv, k_part, v_part, cos, sin)


def q_kernel(shards, normed, wq, part, cos, sin, out):
    width = normed.shape[1]
    mine = pl.ds(pl.multiple_of(shards[2] * width, 128), width)
    raw = part[...] + jnp.dot(normed[...], wq[mine, :], preferred_element_type=jnp.float32)
    for head in range(wq.shape[1] // HD):
        cols = slice(head * HD, head * HD + HD)
        out[:, cols] = rope(raw[:, cols], cos[...], sin[...]).astype(jnp.bfloat16)


def project_q(shards, normed, wq, part, cos, sin):
    rows, width = part.shape
    return pl.pallas_call(
        q_kernel,
        name="project_q",
        out_shape=jax.ShapeDtypeStruct((rows, width), jnp.bfloat16),
        in_specs=[whole(SMEM)] + [whole()] * 5,
        out_specs=whole(),
        compiler_params=pltpu.CompilerParams(vmem_limit_bytes=8 << 20),
        cost_estimate=pl.CostEstimate(
            flops=1000000 * rows, transcendentals=0, bytes_accessed=rows * width
        ),
    )(shards, normed, wq, part, cos, sin)


def attend_kernel(places, first, last, guarded, meta, low_ref, q_ref, *refs):
    count = len(places)
    blocks = refs[:count]
    refs = refs[count:]
    if first:
        acc, tot = refs[-2:]
        acc[...] = jnp.zeros_like(acc)
        tot[...] = jnp.zeros_like(tot)
    else:
        acc_in, tot_in = refs[:2]
        if last:
            out, acc, tot = refs[2:]
            acc[...] = acc_in[...]
            tot[...] = tot_in[...]
        else:
            acc, tot = refs[2:]
    rows = q_ref.shape[0]
    heads = q_ref.shape[1] // HD
    kv_width = blocks[0].shape[1] // 2
    repeat = heads * HD // kv_width

    def visit(block, index, base, top):
        span = SPAN
        key_first = meta[index] + base
        at = slice(top or 0, rows)
        here = (at.stop - at.start, span)
        key_index = key_first + lax.broadcasted_iota(jnp.int32, here, 1)
        allowed = key_index >= jnp.concatenate([low_ref[at, :]] * (span // HD), axis=1)
        if top is not None:
            row = meta[0] + top + lax.broadcasted_iota(jnp.int32, here, 0)
            allowed = allowed & (key_index <= row)
        for head in range(heads):
            cols = slice(head * HD, head * HD + HD)
            group = head // repeat
            keys = block[base : base + span, group * HD : group * HD + HD]
            values = block[
                base : base + span, kv_width + group * HD : kv_width + group * HD + HD
            ]
            raw = lax.dot_general(
                q_ref[at, cols],
                keys,
                (((1,), (1,)), ((), ())),
                preferred_element_type=jnp.float32,
            )
            capped = jnp.tanh(raw * (query_scale / logit_cap))
            weights = jnp.where(allowed, jnp.exp2(capped * (logit_cap * log2e)), 0.0)
            part = weights[:, :HD]
            for k in range(HD, span, HD):
                part = part + weights[:, k : k + HD]
            tot[at, cols] += part
            acc[at, cols] += jnp.dot(
                weights.astype(jnp.bfloat16), values, preferred_element_type=jnp.float32
            )

    def visit_all():
        for block, (index, top) in zip(blocks, places):
            for base in range(0, block.shape[0], SPAN):
                visit(block, index, base, None if top is None else top + base)

    if guarded:
        key_first = meta[places[0][0]]
        pl.when((key_first <= meta[0]) & (key_first + rows > meta[0] - WIN))(visit_all)
    else:
        visit_all()
    if last:
        for head in range(heads):
            cols = slice(head * HD, head * HD + HD)
            total = jnp.sum(tot[:, cols], axis=-1, keepdims=True)
            out[:, cols] = (acc[:, cols] / total).astype(jnp.bfloat16)


def attend(meta, low, queries, parts, state=None, last=False, guarded=False):
    rows, width = queries.shape
    places = tuple((index, top) for _, index, top in parts)
    blocks = [block for block, _, _ in parts]
    wide = jax.ShapeDtypeStruct((rows, width), jnp.float32)
    first = state is None
    operands = [meta, low, queries, *blocks] + ([] if first else list(state))
    keys = sum(block.shape[0] for block in blocks)
    scratch = ()
    aliases = {}
    if last:
        out_shape = jax.ShapeDtypeStruct((rows, width), jnp.bfloat16)
        out_specs = whole()
        scratch = (VMEM((rows, width), jnp.float32), VMEM((rows, width), jnp.float32))
    else:
        out_shape = (wide, wide)
        out_specs = (whole(), whole())
        if not first:
            aliases = {len(operands) - 2: 0, len(operands) - 1: 1}
    return pl.pallas_call(
        functools.partial(attend_kernel, places, first, last, guarded),
        name="attend_last" if last else "attend",
        out_shape=out_shape,
        in_specs=[whole(SMEM)] + [whole()] * (len(operands) - 1),
        out_specs=out_specs,
        scratch_shapes=scratch,
        input_output_aliases=aliases,
        compiler_params=pltpu.CompilerParams(vmem_limit_bytes=8 << 20),
        cost_estimate=pl.CostEstimate(
            flops=3500000 * keys,
            transcendentals=0,
            bytes_accessed=width * keys,
        ),
    )(*operands)


def cache_kernel(shards, *refs):
    out = refs[-1]
    count = len(refs) - 1
    width = refs[0].shape[1] // 2
    for turn, received in enumerate(refs[:-1]):
        shard = shards[(count - turn) % count]
        cols = pl.ds(pl.multiple_of(shard * width, 128), width)
        for index in range(2):
            out[0, :, index, cols] = received[:, index * width : index * width + width]


def exchange_pages(shards, pages):
    count, rows, width = pages.shape
    received = [pages[0]]
    for turn in range(1, count):
        received.append(turned(pages[turn], "tp", turn))
    return pl.pallas_call(
        cache_kernel,
        name="build_cache",
        out_shape=jax.ShapeDtypeStruct((1, rows, 2, count * width // 2), pages.dtype),
        in_specs=[whole(SMEM)] + [whole()] * count,
        out_specs=whole(),
        compiler_params=pltpu.CompilerParams(vmem_limit_bytes=8 << 20),
        cost_estimate=pl.CostEstimate(flops=1000000000, transcendentals=0, bytes_accessed=1000),
    )(shards, *received)


def halves_kernel(left, right, left_out, right_out):
    half = left_out.shape[0]
    left_out[...] = left[:half, :]
    right_out[...] = right[half:, :]


def halves(left, right):
    rows, width = left.shape
    half = jax.ShapeDtypeStruct((rows // 2, width), left.dtype)
    return pl.pallas_call(
        halves_kernel,
        name="halves",
        out_shape=(half, half),
        in_specs=[whole()] * 2,
        out_specs=(whole(), whole()),
        compiler_params=pltpu.CompilerParams(vmem_limit_bytes=8 << 20),
        cost_estimate=pl.CostEstimate(flops=20000000000, transcendentals=0, bytes_accessed=4 * rows * width),
    )(left, right)


def ring_gather(block):
    rows = block.shape[0]
    half = rows // 2
    left = turned(block, "tp", 1)
    right = turned(block, "tp", -1)
    left_half, right_half = halves(left, right)
    far_a = turned(left_half, "tp", 1)
    far_b = turned(right_half, "tp", -1)
    return left, right, (far_a, far_b), left_half


def per_device(hidden, norm_gain, w_query, w_key, w_value, segment_ids, page_table):
    tokens = hidden.shape[0]
    place = lax.axis_index("seq")
    rank = lax.axis_index("tp")
    half = tokens // 2
    ranks = lax.axis_size("tp")
    shards = (rank + jnp.arange(ranks, dtype=jnp.int32)) % ranks
    table = page_table[0]

    left, right, far, forwarded = ring_gather(hidden)
    wide = hidden.astype(jnp.float32)
    with jax.named_scope("far_square"):
        far_square = turned(jnp.sum(wide * wide, axis=-1).reshape(1, tokens), "tp", 2)
    far_square = far_square.reshape(tokens, 1) + jnp.zeros((1, HD), jnp.float32)
    first_token = place * tokens
    steps = WIN // tokens // 2
    core = place % 2
    backs = [jnp.int32(2 * step) for step in range(steps + 1)]
    backs += [2 * step - 1 + 2 * core for step in range(steps + 1)]
    firsts = jnp.stack(backs) * -tokens + first_token
    meta = jnp.concatenate([first_token.reshape(1), firsts, firsts + half])
    later = 2 * (steps + 1)
    marked = (segment_ids + 1).reshape(1, tokens)
    marked, meta = lax.optimization_barrier((marked, meta))
    near = jnp.concatenate(
        [marked, shifted(marked, "seq", 1), shifted(marked, "seq", 2)], axis=0
    )
    earlier = jnp.concatenate(
        [near[1:], shifted(near, "seq", 3), shifted(near, "seq", 6)], axis=0
    ).reshape(1, -1)
    earlier = lax.optimization_barrier((earlier, forwarded))[0]
    own = segment_ids.reshape(tokens, 1) + 1
    before = jnp.sum((marked < own).astype(jnp.int32), axis=1, keepdims=True)
    same = jnp.sum((earlier == own).astype(jnp.int32), axis=1, keepdims=True)
    starts = first_token + before - same
    query_index = first_token + jnp.arange(tokens, dtype=jnp.int32)[:, None]
    low = jnp.maximum(starts, query_index - (WIN - 1)) + jnp.zeros((1, HD), jnp.int32)
    freqs = 10000.0 ** (-(jnp.arange(HD // 2, dtype=jnp.float32) * (2.0 / HD)))
    angles = (query_index - starts).astype(jnp.float32) * jnp.concatenate([freqs, freqs])[None, :]
    sign = np.where(np.arange(HD) < HD // 2, -1.0, 1.0).astype(np.float32)
    cos = jnp.cos(angles)
    sin = jnp.sin(angles) * sign[None, :]
    gain = norm_gain.reshape(1, -1)

    scale, q_part, k_part, v_part = project_early(
        shards, hidden, left, right, far_square, gain, w_query, w_key, w_value
    )
    normed, block, a0, b0, pages = project_kv(
        shards, table, far, scale, gain, w_key, w_value, k_part, v_part, cos, sin
    )

    def after(value, *others):
        return lax.optimization_barrier((value, *others))[0]

    def chain(name, block, ahead):
        arrived = [block]
        for step in range(1, steps + 1):
            moving = after(arrived[-1], ahead) if step == 2 else arrived[-1]
            with jax.named_scope(f"hop_{name}{step}"):
                arrived.append(shifted(moving, "seq", 2))
        return arrived

    def cross(name, block):
        with jax.named_scope(f"cross_{name}"):
            return swapped(block)

    queries = project_q(shards, normed, w_query, q_part, cos, sin)
    a = chain("a", a0, queries)
    b = chain("b", b0, queries)
    look = functools.partial(attend, meta, low)
    straight = [1 + step for step in range(steps + 1)]
    over = [2 + steps + step for step in range(steps + 1)]
    crossed = cross("own", after(block, queries))
    state = look(queries, [(block, straight[0], 0)])
    state = look(queries, [(crossed, over[0], None)], state, guarded=True)
    for step in range(1, steps):
        near, far = straight[step], over[step]
        parts = [
            (a[step], near, None),
            (cross(f"a{step}", a[step]), far, None),
            (b[step], near + later, None),
            (cross(f"b{step}", b[step]), far + later, None),
        ]
        state = look(queries, parts, state)
    kv_cache = exchange_pages(shards, after(pages, b[2]))
    near, far = straight[steps], over[steps]
    edge = [
        (cross(f"a{steps}", a[steps]), far, None),
        (cross(f"b{steps}", after(b[steps], *state, kv_cache)), far + later, None),
    ]
    state = look(queries, [(a[steps], near, None), (b[steps], near + later, None)], state)
    attended = look(queries, edge, state, last=True, guarded=True)
    return (attended, kv_cache)


def solution(mesh):
    placed = (
        P("seq", "tp"),
        P(),
        P(None, "tp"),
        P(None, "tp"),
        P(None, "tp"),
        P("seq"),
        P("seq", None),
    )
    return jax.shard_map(
        per_device,
        mesh=mesh,
        in_specs=placed,
        out_specs=(P("seq", "tp"), P(("seq", "tp"), None, None, None)),
        check_vma=False,
    )
```
